32 devices in a mesh: dp: 32 (over z, y, x, core).
Axes of the slice: x: 2, y: 2, z: 4, core: 2. Of those that a mesh axis runs over, the one named last changes fastest.
Arguments:
- block_in: bfloat16 [4096, 1024], P('dp'), may hold values from -6 to 6
- grad_out: bfloat16 [4096, 1024], P('dp'), may hold values from -6 to 6
- w_qkv: bfloat16 [1024, 3072], P('dp')
- b_qkv: bfloat16 [3072], P('dp'), may hold values from -3 to 3
- w_o: bfloat16 [1024, 1024], P('dp'), may hold values from -1 to 1
- b_o: bfloat16 [1024], P('dp'), may hold values from -2 to 2
- w_in: bfloat16 [1024, 4096], P('dp'), may hold values from -0.1875 to 0.1875
- b_in: bfloat16 [4096], P('dp'), may hold values from -3 to 3
- w_out: bfloat16 [4096, 1024], P('dp'), may hold values from -0.09375 to 0.09375
- b_out: bfloat16 [1024], P('dp'), may hold values from -2 to 2
- ln1_gain: bfloat16 [1024], P('dp'), may hold values from 0.25 to 1.75
- ln1_shift: bfloat16 [1024], P('dp'), may hold values from -2 to 2
- ln2_gain: bfloat16 [1024], P('dp'), may hold values from 0.25 to 1.75
- ln2_shift: bfloat16 [1024], P('dp'), may hold values from -2 to 2
- seq_lens: int32 [96], replicated, may hold values from 0 to 128, as said below
- seq_device: int32 [96], replicated, may hold values from 0 to 31, as said below
- seq_offset: int32 [96], replicated, may hold values from 0 to 128, as said below
Outputs:
- block_out: bfloat16 [4096, 1024], P('dp')
- grad_input: bfloat16 [4096, 1024], P('dp')
- grad_w_qkv: float32 [1024, 3072], P('dp')
- grad_b_qkv: float32 [3072], P('dp')
- grad_w_o: float32 [1024, 1024], P('dp')
- grad_b_o: float32 [1024], P('dp')
- grad_w_in: float32 [1024, 4096], P('dp')
- grad_b_in: float32 [4096], P('dp')
- grad_w_out: float32 [4096, 1024], P('dp')
- grad_b_out: float32 [1024], P('dp')
- grad_ln1_gain: float32 [1024], P('dp')
- grad_ln1_shift: float32 [1024], P('dp')
- grad_ln2_gain: float32 [1024], P('dp')
- grad_ln2_shift: float32 [1024], P('dp')
The draws below stay inside these ranges and needn't reach their ends.
Inputs may be any that keep to these rules, and one draw needn't show every extreme that they name: `seq_lens`: the entries of one device have lengths summing to at most 128; some device holds one entry of exactly 128 tokens; a length of 0 marks an unused entry. `seq_device`: every device holds exactly 3 entries. `seq_offset`: the entries of one device take disjoint runs of slots that start at slot 0 and follow one another without gaps.
All inputs are finite; a program needn't handle non-finite values.
Results may differ from the reference program's by a relative error of at most 0.0087.
Values may be sent and summed in bfloat16 or wider, within the bound.
No kernel may reach another device: no remote copies, remote signals or barrier semaphores. Data moves between devices by JAX's collectives and lax.ppermute only.
A program may use at most 192 MiB of HBM per device.

```python
import math
import jax
import jax.numpy as jnp
from jax import lax

D = 1024
FF = 4096
HEADS = 16
HEAD = 64
ROT = 16
TOK_DEV = 128
SEQ_DEV = 3
TOKENS = 4096
N_DP = 32


def sequence_plan(key):
    load_least = max(TOK_DEV // 16, 4)
    loads = jax.random.randint(jax.random.fold_in(key, 11), (N_DP,), load_least, TOK_DEV + 1)
    full_device = jax.random.randint(jax.random.fold_in(key, 12), (), 0, N_DP)
    filled = jnp.arange(N_DP) == full_device
    loads = jnp.where(filled, TOK_DEV, loads)
    first = jax.random.randint(jax.random.fold_in(key, 13), (N_DP,), 1, loads - 1)
    second = jax.random.randint(jax.random.fold_in(key, 14), (N_DP,), 1, loads - first)
    third = loads - first - second
    first = jnp.where(filled, TOK_DEV, first)
    second = jnp.where(filled, 0, second)
    third = jnp.where(filled, 0, third)
    lengths = jnp.stack([first, second, third], axis=1).reshape(-1)
    offsets = jnp.stack([jnp.zeros_like(first), first, first + second], axis=1).reshape(-1)
    owners = jnp.repeat(jnp.arange(N_DP, dtype=jnp.int32), SEQ_DEV)
    order = jax.random.permutation(jax.random.fold_in(key, 15), N_DP * SEQ_DEV)
    return (lengths[order].astype(jnp.int32), owners[order].astype(jnp.int32), offsets[order].astype(jnp.int32))


def draw_seq_lens(key, part):
    return sequence_plan(key)[0]


def draw_seq_device(key, part):
    return sequence_plan(key)[1]


def draw_seq_offset(key, part):
    return sequence_plan(key)[2]


def draw_w_qkv(key, part):
    base = jax.random.normal(jax.random.fold_in(key, 21), (D, 3 * D), jnp.float32)
    return (base * (1.0 / math.sqrt(D))).astype(jnp.bfloat16)


def levels(rng, dims, shards, low, largest):
    def one(axis_at, blocks):
        draws = jax.random.uniform(jax.random.fold_in(jax.random.fold_in(rng, 6), axis_at), (blocks,), jnp.float32, low / len(shards), largest / len(shards))
        return jnp.repeat(jnp.exp(draws), dims[axis_at] // blocks).reshape((-1,) + (1,) * (len(dims) - axis_at - 1))

    level = one(*shards[0])
    for cut in shards[1:]:
        level = level * one(*cut)
    return level


def centred(own_key, extent, scale, limit, shards=(), held_as=jnp.bfloat16):
    drawn = scale * jax.random.normal(own_key, extent, jnp.float32)
    if shards:
        drawn = drawn * levels(own_key, extent, shards, -0.22, 0.18)
    return jnp.clip(drawn, -limit, limit).astype(held_as)


def setup_inputs(seed: int = 0) -> dict:
    streams_of = jax.random.split(jax.random.key(seed), 18)
    return {
        "block_in": centred(streams_of[0], (TOKENS, D), 1.0, 6.0, ((0, 32),)),
        "grad_out": centred(streams_of[1], (TOKENS, D), 1.0, 6.0, ((0, 32),)),
        "w_qkv": draw_w_qkv(jax.random.fold_in(streams_of[17], 71), 0),
        "b_qkv": centred(streams_of[3], (3 * D,), 0.5, 3.0, ((0, 32),)),
        "w_o": centred(streams_of[4], (D, D), (D // 32) ** -0.5, 1.0, ((0, 32),)),
        "b_o": centred(streams_of[5], (D,), 0.3, 2.0, ((0, 32),)),
        "w_in": centred(streams_of[6], (D, FF), D ** -0.5, 0.1875, ((0, 32),)),
        "b_in": centred(streams_of[7], (FF,), 0.5, 3.0, ((0, 32),)),
        "w_out": centred(streams_of[8], (FF, D), FF ** -0.5, 0.09375, ((0, 32),)),
        "b_out": centred(streams_of[9], (D,), 0.3, 2.0, ((0, 32),)),
        "ln1_gain": jnp.clip(1.0 + 0.15 * jax.random.normal(streams_of[10], (D,), jnp.float32), 0.25, 1.75).astype(jnp.bfloat16),
        "ln1_shift": centred(streams_of[11], (D,), 0.3, 2.0, ((0, 32),)),
        "ln2_gain": jnp.clip(1.0 + 0.15 * jax.random.normal(streams_of[12], (D,), jnp.float32), 0.25, 1.75).astype(jnp.bfloat16),
        "ln2_shift": centred(streams_of[13], (D,), 0.3, 2.0, ((0, 32),)),
        "seq_lens": draw_seq_lens(jax.random.fold_in(streams_of[17], 71), 0),
        "seq_device": draw_seq_device(jax.random.fold_in(streams_of[17], 71), 0),
        "seq_offset": draw_seq_offset(jax.random.fold_in(streams_of[17], 71), 0),
    }


highest = lax.Precision.HIGHEST

@jax.custom_vjp
def low(v):
    return lax.optimization_barrier(v.astype(jnp.bfloat16)).astype(jnp.float32)

@jax.custom_vjp
def low_back(v):
    return v

def low_keep(v):
    return (low(v), None)

def low_pass(kept, grad):
    return (grad,)

def back_keep(v):
    return (v, None)

def back_low(kept, grad):
    return (low(grad),)
low.defvjp(low_keep, low_pass)
low_back.defvjp(back_keep, back_low)

def times_high(left, right):
    return jnp.dot(left, right, precision=highest, preferred_element_type=jnp.float32)

def norm_rows(values, gain, shift):
    centre = lax.optimization_barrier(jnp.mean(values, axis=-1, keepdims=True))
    centered = values - centre
    spread = lax.optimization_barrier(jnp.mean(centered * centered, axis=-1, keepdims=True))
    return centered * lax.rsqrt(spread + 1e-05) * gain + shift

def rotate(heads_in, cosine, sines):
    half = cosine.shape[-1]
    first = heads_in[..., :half]
    second = heads_in[..., half:2 * half]
    return jnp.concatenate([first * cosine - second * sines, second * cosine + first * sines, heads_in[..., 2 * half:]], axis=-1)

def angles(position, rotary):
    half = rotary // 2
    freqs = 10000.0 ** (-jnp.arange(half, dtype=jnp.float32) / half)
    angle = position.astype(jnp.float32)[:, None] * freqs[None, :]
    return (jnp.cos(angle)[:, None, :], jnp.sin(angle)[:, None, :])

def layout(device, slots, seq_lens, seq_device, seq_offset):
    count = seq_lens.shape[0]
    inside = (seq_device[None, :] == device[:, None]) & (slots[:, None] >= seq_offset[None, :]) & (slots[:, None] < (seq_offset + seq_lens)[None, :])
    number = jnp.arange(count, dtype=jnp.int32)
    present = jnp.any(inside, axis=1)
    segment = lax.optimization_barrier(jnp.sum(jnp.where(inside, number[None, :], 0), axis=1)).astype(jnp.int32)
    segment = jnp.where(present, segment, count + slots).astype(jnp.int32)
    position = lax.optimization_barrier(jnp.sum(jnp.where(inside, slots[:, None] - seq_offset[None, :], 0), axis=1)).astype(jnp.int32)
    return (present.astype(jnp.float32), segment, position)

def layer_rows(inputs, params, live, segment, position):
    w_qkv, b_qkv, w_o, b_o, w_in, b_in, w_out, b_out, gain_one, shift_one, gain_two, shift_two = params
    row_count = inputs.shape[0]
    buffers = row_count // TOK_DEV
    act_one = low(norm_rows(inputs, gain_one, shift_one))
    act_two = low(norm_rows(inputs, gain_two, shift_two))
    qkv = low_back(times_high(act_one, w_qkv) + b_qkv)
    cosine, sines = angles(position, ROT)
    query = low(rotate(qkv[:, :D].reshape(row_count, HEADS, HEAD), cosine, sines)).reshape(buffers, TOK_DEV, HEADS, HEAD)
    keys = low(rotate(qkv[:, D:2 * D].reshape(row_count, HEADS, HEAD), cosine, sines)).reshape(buffers, TOK_DEV, HEADS, HEAD)
    values = low(qkv[:, 2 * D:]).reshape(buffers, TOK_DEV, HEADS, HEAD)
    seg_blocks = segment.reshape(buffers, TOK_DEV)
    slots = jnp.arange(TOK_DEV, dtype=jnp.int32)
    allowed = (seg_blocks[:, :, None] == seg_blocks[:, None, :]) & (slots[None, None, :] <= slots[None, :, None])
    scores = low_back(jnp.einsum('bqhd,bkhd->bhqk', query, keys, precision=highest, preferred_element_type=jnp.float32) / math.sqrt(HEAD))
    scores = jnp.where(allowed[:, None], scores, -1e+30)
    attn_probs = low(jnp.exp(scores - jax.nn.logsumexp(scores, axis=-1, keepdims=True)))
    mixed = jnp.einsum('bhqk,bkhd->bqhd', attn_probs, values, precision=highest, preferred_element_type=jnp.float32).reshape(row_count, D)
    mixed = low_back(low(mixed))
    attended = low_back(times_high(mixed, w_o) + b_o)
    hidden_pre = low_back(times_high(act_two, w_in) + b_in)
    hidden = low(jax.nn.gelu(hidden_pre, approximate=False))
    mapped = low_back(times_high(hidden, w_out) + b_out)
    return live[:, None] * (inputs + attended + mapped)

def reference(block_in, grad_out, w_qkv, b_qkv, w_o, b_o, w_in, b_in, w_out, b_out, ln1_gain, ln1_shift, ln2_gain, ln2_shift, seq_lens, seq_device, seq_offset):
    group_size = 8
    groups = N_DP // group_size
    group_rows = group_size * TOK_DEV
    rows_all = jnp.arange(TOKENS, dtype=jnp.int32)
    device = (rows_all // TOK_DEV).astype(jnp.int32)
    slots = (rows_all % TOK_DEV).astype(jnp.int32)
    live, segment, position = layout(device, slots, seq_lens, seq_device, seq_offset)
    params = tuple((member.astype(jnp.float32) for member in (w_qkv, b_qkv, w_o, b_o, w_in, b_in, w_out, b_out, ln1_gain, ln1_shift, ln2_gain, ln2_shift)))

    def forward(inputs, weights):

        def one_group(pieces):
            return layer_rows(pieces[0], weights, pieces[1], pieces[2], pieces[3])
        stacked = lax.map(jax.checkpoint(one_group), (inputs.reshape(groups, group_rows, D), live.reshape(groups, group_rows), segment.reshape(groups, group_rows), position.reshape(groups, group_rows)))
        return stacked.reshape(TOKENS, D)
    result, pullback = jax.vjp(forward, block_in.astype(jnp.float32), params)
    grad_x, grads = pullback(grad_out.astype(jnp.float32))
    return (result.astype(jnp.bfloat16), grad_x.astype(jnp.bfloat16), grads[0], grads[1], grads[2], grads[3], grads[4], grads[5], grads[6], grads[7], grads[8], grads[9], grads[10], grads[11])
```

```python
import math

import jax
import jax.numpy as jnp
from jax import lax
from jax.sharding import PartitionSpec as P

D = 1024
HEADS = 16
HEAD = 64
ROT = 16
NB = 4

F32 = jnp.float32
BF = jnp.bfloat16


def dot_nn(left, right):
    return jnp.dot(left, right, preferred_element_type=F32)


def dot_nt(left, right):
    return lax.dot_general(left, right, (((1,), (1,)), ((), ())), preferred_element_type=F32)


def dot_tn(left, right):
    return lax.dot_general(left, right, (((0,), (0,)), ((), ())), preferred_element_type=F32)


def rotate(heads_in, cosine, sines):
    half = cosine.shape[-1]
    first = heads_in[..., :half]
    second = heads_in[..., half : 2 * half]
    return jnp.concatenate(
        [first * cosine - second * sines, second * cosine + first * sines, heads_in[..., 2 * half :]],
        axis=-1,
    )


def layout(device, slots, seq_lens, seq_device, seq_offset):
    count = seq_lens.shape[0]
    inside = (
        (seq_device[None, :] == device[:, None])
        & (slots[:, None] >= seq_offset[None, :])
        & (slots[:, None] < (seq_offset + seq_lens)[None, :])
    )
    number = jnp.arange(count, dtype=jnp.int32)
    present = jnp.any(inside, axis=1)
    segment = jnp.sum(jnp.where(inside, number[None, :], 0), axis=1)
    segment = jnp.where(present, segment, count + slots)
    position = jnp.sum(jnp.where(inside, slots[:, None] - seq_offset[None, :], 0), axis=1)
    return (present.astype(F32), segment, position)


def make(n):
    R = n // NB
    bits = R.bit_length() - 1
    assert R * NB == n and 1 << bits == R

    def shift(v, k):
        k = k % NB
        return lax.ppermute(v, "dp", [(b * R + r, (b + k) % NB * R + r) for b in range(NB) for r in range(R)])

    def swap(v, mask):
        return lax.ppermute(v, "dp", [(d, d ^ mask) for d in range(n)])

    def gather_r(own):
        got = {0: own}
        if bits == 3:
            from_x, from_y = swap(own, 2), swap(own, 4)
            half = own.shape[0] // 2
            low = swap(from_x[:half], 4)
            high = swap(from_y[half:], 2)
            got = {0: own, 2: from_x, 4: from_y, 6: jnp.concatenate([low, high])}
        else:
            for k in range(1, bits):
                for m, v in list(got.items()):
                    got[m ^ (1 << k)] = swap(v, 1 << k)
        for m, v in list(got.items()):
            got[m ^ 1] = swap(v, 1)
        return got

    def scatter_r(part):
        kept = {}
        for m in range(0, R, 2):
            kept[m] = part(m) + swap(part(m ^ 1).astype(BF), 1).astype(F32)
        if bits == 3:
            half = kept[6].shape[0] // 2
            low = swap(kept[6][:half].astype(BF), 2).astype(F32)
            high = swap(kept[6][half:].astype(BF), 4).astype(F32)
            to_y = jnp.concatenate([kept[4][:half] + low, kept[4][half:]])
            to_x = jnp.concatenate([kept[2][:half], kept[2][half:] + high])
            return kept[0] + swap(to_x.astype(BF), 2).astype(F32) + swap(to_y.astype(BF), 4).astype(F32)
        for k in reversed(range(1, bits)):
            for m in [m for m in kept if m < 1 << k]:
                kept[m] = kept[m] + swap(kept.pop(m ^ (1 << k)).astype(BF), 1 << k).astype(F32)
        return kept[0]

    def on_device(
        block_in, grad_out, w_qkv, b_qkv, w_o, b_o, w_in, b_in, w_out, b_out,
        ln1_gain, ln1_shift, ln2_gain, ln2_shift, seq_lens, seq_device, seq_offset,
    ):
        T = block_in.shape[0]
        rows = w_qkv.shape[0]
        ff_dev = w_out.shape[0]
        HB = HEADS // NB
        QB = D // NB
        FB = w_in.shape[1] // NB
        idx = lax.axis_index("dp")
        b, r = idx // R, idx % R

        slots1 = jnp.arange(T, dtype=jnp.int32)
        owners = [(b - k) % NB * R + r for k in range(NB)]
        device = jnp.concatenate([jnp.full((T,), o, jnp.int32) for o in owners])
        slots = jnp.tile(slots1, NB)
        live, segment, position = layout(device, slots, seq_lens, seq_device, seq_offset)
        live_own = live[:T]
        seg = segment.reshape(NB, T)
        allowed = (seg[:, :, None] == seg[:, None, :]) & (slots1[None, None, :] <= slots1[None, :, None])
        half = ROT // 2
        freqs = 10000.0 ** (-jnp.arange(half, dtype=F32) / half)
        angle = position.astype(F32)[:, None] * freqs[None, :]
        cosine, sines = jnp.cos(angle)[:, None, :], jnp.sin(angle)[:, None, :]

        def columns(k):
            to = (b + k) % NB
            q = lax.dynamic_slice_in_dim(w_qkv.reshape(rows, 3, NB, QB), to, 1, 2).reshape(rows, 3 * QB)
            return jnp.concatenate([q, lax.dynamic_slice_in_dim(w_in, to * FB, FB, 1)], axis=1)

        mine = jnp.zeros((NB, rows, 3 * QB + FB), BF)
        for k in range(NB):
            got = columns(0) if k == 0 else shift(columns(k), k)
            mine = lax.dynamic_update_slice(mine, got[None], ((b - k) % NB, 0, 0))

        tokens = jnp.concatenate([block_in] + [shift(block_in, k) for k in range(1, NB)])
        grad_own = live_own[:, None] * grad_out.astype(F32)
        grad_own_r = grad_own.astype(BF)
        grad_r = jnp.concatenate([grad_own_r] + [shift(grad_own_r, k) for k in range(1, NB)])

        small = [b_qkv, b_o, b_in, b_out, ln1_gain, ln1_shift, ln2_gain, ln2_shift]
        sizes = [v.shape[0] for v in small]
        packed = jnp.concatenate(small)
        packed = lax.all_to_all(jnp.broadcast_to(packed[None], (n, packed.shape[0])), "dp", 0, 0, tiled=True)
        vectors, at = [], 0
        for size in sizes:
            vectors.append(packed[:, at : at + size].reshape(-1).astype(F32))
            at += size
        bias_qkv, bias_o, bias_in, bias_out, gain_one, shift_one, gain_two, shift_two = vectors
        bias_qkv = lax.dynamic_slice_in_dim(bias_qkv.reshape(3, NB, QB), b, 1, 1).reshape(3 * QB)
        bias_in = lax.dynamic_slice_in_dim(bias_in, b * FB, FB)

        pieces_two = gather_r(jnp.concatenate([w_o, w_out]))
        full_o = jnp.zeros((R, rows, D), BF)
        full_out = jnp.zeros((R, ff_dev, D), BF)
        for m, v in pieces_two.items():
            full_o = lax.dynamic_update_slice(full_o, v[None, :rows], (r ^ m, 0, 0))
            full_out = lax.dynamic_update_slice(full_out, v[None, rows:], (r ^ m, 0, 0))
        full_o, full_out = full_o.reshape(R * rows, D), full_out.reshape(R * ff_dev, D)
        pieces_one = gather_r(mine)
        full_one = jnp.zeros((NB, R, rows, 3 * QB + FB), BF)
        for m, v in pieces_one.items():
            full_one = lax.dynamic_update_slice(full_one, v[:, None], (0, r ^ m, 0, 0))
        full_one = full_one.reshape(D, 3 * QB + FB)
        full_qkv, full_in = full_one[:, : 3 * QB], full_one[:, 3 * QB :]

        inputs = tokens.astype(F32)
        centre = jnp.mean(inputs, axis=-1, keepdims=True)
        centered = inputs - centre
        spread = jnp.mean(centered * centered, axis=-1, keepdims=True)
        rstd = lax.rsqrt(spread + 1e-05)
        xhat = centered * rstd
        act_one = (xhat * gain_one + shift_one).astype(BF)
        act_two = (xhat * gain_two + shift_two).astype(BF)
        qkv = dot_nn(act_one, full_qkv) + bias_qkv
        NT = NB * T
        query = rotate(qkv[:, :QB].reshape(NT, HB, HEAD), cosine, sines)
        keys = rotate(qkv[:, QB : 2 * QB].reshape(NT, HB, HEAD), cosine, sines)
        query_r = query.astype(BF).reshape(NB, T, HB, HEAD)
        keys_r = keys.astype(BF).reshape(NB, T, HB, HEAD)
        values_r = qkv[:, 2 * QB :].astype(BF).reshape(NB, T, HB, HEAD)
        scores = jnp.einsum("bqhd,bkhd->bhqk", query_r, keys_r, preferred_element_type=F32) / math.sqrt(HEAD)
        scores = jnp.where(allowed[:, None], scores, -1e30)
        log_total = jax.nn.logsumexp(scores, axis=-1, keepdims=True)
        probs = jnp.exp(scores - log_total)
        probs_r = probs.astype(BF)
        mixed_r = (
            jnp.einsum("bhqk,bkhd->bqhd", probs_r, values_r, preferred_element_type=F32).reshape(NT, QB).astype(BF)
        )
        hid_pre = dot_nn(act_two, full_in) + bias_in
        cdf = 0.5 * (1.0 + lax.erf(hid_pre * (1.0 / math.sqrt(2.0))))
        hidden_r = (hid_pre * cdf).astype(BF)
        part_out = dot_nn(mixed_r, full_o) + dot_nn(hidden_r, full_out)
        total = block_in.astype(F32) + bias_o + bias_out + part_out[:T]
        for k in range(1, NB):
            total = total + shift(part_out[k * T : (k + 1) * T].astype(BF), -k).astype(F32)
        block_out = (live_own[:, None] * total).astype(BF)

        term_o = dot_tn(mixed_r, grad_r).reshape(R, rows, D)
        term_out = dot_tn(hidden_r, grad_r).reshape(R, ff_dev, D)

        def part_two(m):
            return jnp.concatenate(
                [
                    lax.dynamic_index_in_dim(term_o, r ^ m, 0, keepdims=False),
                    lax.dynamic_index_in_dim(term_out, r ^ m, 0, keepdims=False),
                ]
            )

        grad_two = scatter_r(part_two)
        grad_w_o, grad_w_out = grad_two[:rows], grad_two[rows:]
        d_mixed_r = dot_nt(grad_r, full_o).astype(BF).reshape(NB, T, HB, HEAD)
        d_hidden = dot_nt(grad_r, full_out)
        pdf = jnp.exp(-0.5 * hid_pre * hid_pre) * (1.0 / math.sqrt(2.0 * math.pi))
        d_hidden_pre_r = (d_hidden * (cdf + hid_pre * pdf)).astype(BF)
        d_probs = jnp.einsum("bqhd,bkhd->bhqk", d_mixed_r, values_r, preferred_element_type=F32)
        delta = jnp.sum(d_probs * probs, axis=-1, keepdims=True)
        d_scores_r = (probs * (d_probs - delta)).astype(BF)
        d_query = jnp.einsum("bhqk,bkhd->bqhd", d_scores_r, keys_r, preferred_element_type=F32) / math.sqrt(HEAD)
        d_keys = jnp.einsum("bhqk,bqhd->bkhd", d_scores_r, query_r, preferred_element_type=F32) / math.sqrt(HEAD)
        d_values = jnp.einsum("bhqk,bqhd->bkhd", probs_r, d_mixed_r, preferred_element_type=F32)
        d_query_pre = rotate(d_query.reshape(NT, HB, HEAD), cosine, -sines)
        d_keys_pre = rotate(d_keys.reshape(NT, HB, HEAD), cosine, -sines)
        d_qkv_r = jnp.concatenate(
            [d_query_pre.reshape(NT, QB), d_keys_pre.reshape(NT, QB), d_values.reshape(NT, QB)], axis=1
        ).astype(BF)
        term_one = jnp.concatenate([dot_tn(act_one, d_qkv_r), dot_tn(act_two, d_hidden_pre_r)], axis=1)
        term_one = term_one.reshape(NB, R, rows, 3 * QB + FB)

        def part_one(m):
            return lax.dynamic_index_in_dim(term_one, r ^ m, 1, keepdims=False)

        grad_one = scatter_r(part_one)
        grad_w_qkv = jnp.zeros((rows, 3, NB, QB), F32)
        grad_w_in = jnp.zeros((rows, NB * FB), F32)
        for k in range(NB):
            to = (b - k) % NB
            got = lax.dynamic_index_in_dim(grad_one, to, 0, keepdims=False)
            if k:
                got = shift(got.astype(BF), -k).astype(F32)
            at = (b + k) % NB
            grad_w_qkv = lax.dynamic_update_slice(grad_w_qkv, got[:, : 3 * QB].reshape(rows, 3, 1, QB), (0, 0, at, 0))
            grad_w_in = lax.dynamic_update_slice(grad_w_in, got[:, 3 * QB :], (0, at * FB))
        grad_w_qkv = grad_w_qkv.reshape(rows, 3 * D)

        d_act_one = dot_nt(d_qkv_r, full_qkv)
        d_act_two = dot_nt(d_hidden_pre_r, full_in)
        g_part = d_act_one * gain_one + d_act_two * gain_two
        g = g_part[:T]
        for k in range(1, NB):
            g = g + shift(g_part[k * T : (k + 1) * T].astype(BF), -k).astype(F32)
        xhat_own, rstd_own = xhat[:T], rstd[:T]
        mean_g = jnp.mean(g, axis=-1, keepdims=True)
        mean_gx = jnp.mean(g * xhat_own, axis=-1, keepdims=True)
        grad_input = (grad_own + rstd_own * (g - mean_g - xhat_own * mean_gx)).astype(BF)

        sum_qkv = jnp.sum(d_qkv_r.astype(F32), axis=0).reshape(3, 1, QB)
        sum_qkv = lax.dynamic_update_slice(jnp.zeros((3, NB, QB), F32), sum_qkv, (0, b, 0)).reshape(n, -1)
        sum_in = jnp.sum(d_hidden_pre_r.astype(F32), axis=0)
        sum_in = lax.dynamic_update_slice(jnp.zeros((NB * FB,), F32), sum_in, (b * FB,)).reshape(n, -1)
        sums = [
            sum_qkv,
            sum_in,
            jnp.sum(grad_own_r.astype(F32), axis=0).reshape(n, -1),
            jnp.sum(d_act_one * xhat, axis=0).reshape(n, -1),
            jnp.sum(d_act_one, axis=0).reshape(n, -1),
            jnp.sum(d_act_two * xhat, axis=0).reshape(n, -1),
            jnp.sum(d_act_two, axis=0).reshape(n, -1),
        ]
        widths = [s.shape[1] for s in sums]
        summed = jnp.sum(lax.all_to_all(jnp.concatenate(sums, axis=1), "dp", 0, 0, tiled=True), axis=0)
        outs, at = [], 0
        for width in widths:
            outs.append(summed[at : at + width])
            at += width
        grad_b_qkv, grad_b_in, grad_b, grad_g1, grad_s1, grad_g2, grad_s2 = outs
        return (
            block_out, grad_input, grad_w_qkv, grad_b_qkv, grad_w_o, grad_b, grad_w_in, grad_b_in,
            grad_w_out, grad_b, grad_g1, grad_s1, grad_g2, grad_s2,
        )

    return on_device


def solution(mesh):
    two, one = P("dp", None), P("dp")
    return jax.shard_map(
        make(mesh.shape["dp"]),
        mesh=mesh,
        in_specs=(two, two, two, one, two, one, two, one, two, one, one, one, one, one, P(), P(), P()),
        out_specs=(two, two, two, one, two, one, two, one, two, one, one, one, one, one),
        check_vma=False,
    )
```

```python
import math

import jax
import jax.numpy as jnp
from jax import lax
from jax.experimental import pallas as pl
from jax.experimental.pallas import tpu as pltpu
from jax.sharding import PartitionSpec as P


D = 1024
HEAD = 64
ROT = 16
NB = 4
QB = D // NB
NEG = -1e30

F32 = jnp.float32
BF = jnp.bfloat16
I32 = jnp.int32


def dot_nn(left, right):
    return jnp.dot(left, right, preferred_element_type=F32)


def dot_nt(left, right):
    return lax.dot_general(left, right, (((1,), (1,)), ((), ())), preferred_element_type=F32)


def iota(shape, axis):
    return lax.broadcasted_iota(I32, shape, axis)


def call(body, ins, outs, scratch=(), flops=0, extra=4 << 20, hbm=()):
    spaces = {"v": pltpu.VMEM, "s": pltpu.SMEM, "a": pl.ANY}
    arrays = [a for _, a in ins]
    nbytes = sum(a.size * a.dtype.itemsize for a in arrays) + sum(math.prod(o.shape) * o.dtype.itemsize for o in outs)
    room = sum(math.prod(t.shape) * jnp.dtype(t.dtype).itemsize for t in scratch if t.memory_space == pltpu.VMEM)
    room += sum(a.size * a.dtype.itemsize for s, a in ins if s == "v") + sum(math.prod(o.shape) * o.dtype.itemsize for i, o in enumerate(outs) if i not in hbm)
    return pl.pallas_call(
        body,
        out_shape=tuple(outs),
        in_specs=[pl.BlockSpec(memory_space=spaces[s]) for s, _ in ins],
        out_specs=tuple(pl.BlockSpec(memory_space=pltpu.HBM if i in hbm else pltpu.VMEM) for i in range(len(outs))),
        scratch_shapes=list(scratch),
        compiler_params=pltpu.CompilerParams(vmem_limit_bytes=int(room * 1.02) + extra),
        cost_estimate=pl.CostEstimate(flops=int(flops), bytes_accessed=int(nbytes), transcendentals=0),
    )(*arrays)


def sds(shape, dtype):
    return jax.ShapeDtypeStruct(shape, dtype)


def by_rows(count, chunk, fn):
    def step(i, carry):
        fn(pl.ds(pl.multiple_of(i * chunk, chunk), chunk))
        return carry

    lax.fori_loop(0, count // chunk, step, 0)


def lanes(i, width):
    return pl.ds(pl.multiple_of(i * width, width), width)


def partner(v):
    low = iota(v.shape, 1) % HEAD < ROT // 2
    return jnp.where(low, pltpu.roll(v, v.shape[1] - ROT // 2, 1), pltpu.roll(v, ROT // 2, 1))


def split_heads(v):
    first = iota(v.shape, 1) < HEAD
    zero = jnp.zeros_like(v)
    return jnp.concatenate([jnp.where(first, v, zero), jnp.where(first, zero, v)], axis=0)


def stats(x):
    centre = jnp.mean(x, axis=-1, keepdims=True)
    centered = x - centre
    spread = jnp.mean(centered * centered, axis=-1, keepdims=True)
    return centered, lax.rsqrt(spread + 1e-05)


def make(n):
    R = n // NB
    assert R * NB == n and R & (R - 1) == 0

    def shift(v, k):
        k = k % NB
        return lax.ppermute(v, "dp", [(b * R + r, (b + k) % NB * R + r) for b in range(NB) for r in range(R)])

    def swap(v, mask):
        return lax.ppermute(v, "dp", [(d, d ^ mask) for d in range(n)])

    def gather_r(own):
        got = {0: own}
        for m in range(2, R, 2):
            got[m] = swap(own, m)
        for m in range(0, R, 2):
            got[m + 1] = swap(got[m], 1)
        return [got[m] for m in range(R)]

    def on_device(
        block_in, grad_out, w_qkv, b_qkv, w_o, b_o, w_in, b_in, w_out, b_out,
        ln1_gain, ln1_shift, ln2_gain, ln2_shift, seq_lens, seq_device, seq_offset,
    ):
        T = block_in.shape[0]
        NT = NB * T
        rows = w_qkv.shape[0]
        ff_dev = w_out.shape[0]
        FB = w_in.shape[1] // NB
        W1 = 3 * QB + FB
        J = R // 2
        MF = NB * rows + ff_dev
        MA = NB * rows
        idx = lax.axis_index("dp").astype(I32)
        b, r = idx // R, idx % R
        br = jnp.stack([b, r])

        slots1 = jnp.arange(T, dtype=I32)
        owners = [(b - k) % NB * R + r for k in range(NB)]
        device = jnp.concatenate([jnp.full((T,), o, I32) for o in owners])
        slots = jnp.tile(slots1, NB)
        count = seq_lens.shape[0]
        inside = (
            (seq_device[None, :] == device[:, None])
            & (slots[:, None] >= seq_offset[None, :])
            & (slots[:, None] < (seq_offset + seq_lens)[None, :])
        )
        number = jnp.arange(count, dtype=I32)
        present = jnp.any(inside, axis=1)
        segment = jnp.where(present, jnp.sum(jnp.where(inside, number[None, :], 0), axis=1), count + slots)
        position = jnp.sum(jnp.where(inside, slots[:, None] - seq_offset[None, :], 0), axis=1)
        live = present.astype(F32)[:, None]
        seg = segment.reshape(NB, T)
        allowed = (seg[:, :, None] == seg[:, None, :]) & (slots1[None, None, :] <= slots1[None, :, None])
        mask = jnp.where(allowed, 0.0, NEG).astype(F32)
        lane = jnp.arange(2 * HEAD, dtype=I32) % HEAD
        half = ROT // 2
        freqs = 10000.0 ** (-(lane % half).astype(F32) / half)
        angle = position.astype(F32)[:, None] * jnp.where(lane < ROT, freqs, 0.0)[None, :]
        cosine = jnp.cos(angle)
        sines = jnp.sin(angle) * jnp.where(lane < half, -1.0, 1.0)[None, :]

        small = [b_in, b_qkv, b_o, b_out, ln1_gain, ln1_shift, ln2_gain, ln2_shift]
        widths = [v.shape[0] for v in small]
        offsets = [sum(widths[:i]) for i in range(len(small))]
        WS = 1024

        def pack_body(br, qkv_ref, in_ref, o_ref, out_ref, *rest):
            vectors, outs = rest[: len(small)], rest[len(small) :]
            for k in range(NB):
                to = lax.rem(br[0] + k, NB)
                for s in range(3):
                    outs[k][:, s * QB : (s + 1) * QB] = qkv_ref[:, lanes(s * NB + to, QB)]
                outs[k][:, 3 * QB :] = in_ref[:, lanes(to, FB)]
            outs[NB][:ff_dev] = out_ref[...]
            outs[NB][ff_dev:] = o_ref[...]
            parts = [v[...].astype(F32) for v in vectors]
            if WS > sum(widths):
                parts.append(jnp.zeros((1, WS - sum(widths)), F32))
            every = jnp.concatenate(parts, axis=1)
            for i in range(8):
                outs[NB + 1][:, i] = jnp.broadcast_to(every[:, i * 128 : (i + 1) * 128], (n, 128)).astype(BF)

        packed = call(
            pack_body,
            [("s", br), ("v", w_qkv), ("v", w_in), ("v", w_o), ("v", w_out)] + [("v", v.reshape(1, -1)) for v in small],
            [sds((rows, W1), BF)] * NB + [sds((ff_dev + rows, D), BF), sds((n, 8, 128), BF)], extra=56 << 20,
        )
        columns, own_two, small_out = packed[:NB], packed[NB], packed[NB + 1]

        mine = jnp.concatenate([columns[0]] + [shift(columns[k], k) for k in range(1, NB)]).reshape(NB, rows, W1)
        two = gather_r(own_two)
        one = gather_r(mine)
        after, _ = lax.optimization_barrier((block_in, mine))
        tokens = [block_in] + [shift(after, k) for k in range(1, NB)]
        small_in = lax.all_to_all(small_out, "dp", 0, 0, tiled=True)
        after, _ = lax.optimization_barrier((grad_out, tokens))
        grads_in = [grad_out] + [shift(after, k) for k in range(1, NB)]

        def pick(width_mod, off, base, width):
            return (iota((width, width_mod.shape[1]), 0) + base == off + width_mod).astype(BF)

        def window(off, width):
            base = off // 128 * 128
            return base, -(-(off + width) // 128) * 128 - base

        def dec_body(br, got, bq, bi, g1, s1, g2, s2, bo):
            def expand(which, col):
                width, off = widths[which], offsets[which]
                base, span = window(off, width)
                total = col.shape[1]
                sel = pick(lax.rem(col, width), off, base, span)
                every = dot_nn(jnp.concatenate([got[:, i] for i in range(base // 128, (base + span) // 128)], axis=1), sel)
                return jnp.sum(jnp.where(iota((n, total), 0) == lax.div(col, width), every, 0.0), axis=0, keepdims=True)

            at = iota((1, 3 * QB), 1)
            bq[...] = expand(1, lax.div(at, QB) * D + br[0] * QB + lax.rem(at, QB))
            bi[...] = expand(0, iota((1, FB), 1) + br[0] * FB)
            whole = iota((1, D), 1)
            bo[...] = expand(2, whole) + expand(3, whole)
            for ref, which in ((g1, 4), (s1, 5), (g2, 6), (s2, 7)):
                ref[...] = expand(which, whole)

        row = sds((1, D), F32)
        bias_qkv, bias_in, gain_one, shift_one, gain_two, shift_two, bias_o = call(
            dec_body, [("s", br), ("v", small_in)], [sds((1, 3 * QB), F32), sds((1, FB), F32)] + [row] * 5
        )

        def load_one(br, pieces, w1, sems):
            copies = []
            for m in range(R):
                for k in range(NB):
                    copies.append(
                        pltpu.make_async_copy(
                            pieces[m].at[k], w1.at[lax.rem(br[0] + (NB - k), NB), br[1] ^ m], sems.at[m * NB + k]
                        )
                    )
            return copies

        def load_out(br, pieces, wout, sems):
            return [
                pltpu.make_async_copy(pieces[m].at[pl.ds(0, ff_dev)], wout.at[br[1] ^ m], sems.at[m]) for m in range(R)
            ]

        def load_o(br, pieces, wo, sems):
            return [
                pltpu.make_async_copy(pieces[m].at[pl.ds(ff_dev, rows)], wo.at[br[1] ^ m], sems.at[m]) for m in range(R)
            ]

        dma = pltpu.SemaphoreType.DMA
        PAIRS = QB // 128

        def fwd_body(br, x0, x1, x2, x3, cos, sin, mask_ref, bq, bi, g1, s1, g2, s2, *rest):
            one, two, rest = rest[:R], rest[R : 2 * R], rest[2 * R :]
            act1, act2, q, k, v, probs, mixed, hidden, dgelu, xhat_ref, w1, wo, wout, own, p1h, p2h, p3h = rest[:17]
            p1, p2, p3, sem1, semo, semout, semp = rest[17:]
            c1, co, cout = load_one(br, one, w1, sem1), load_o(br, two, wo, semo), load_out(br, two, wout, semout)
            for c in c1 + co + cout:
                c.start()
            for i, x in enumerate((x0, x1, x2, x3)):

                def norm(rws, i=i, x=x):
                    centered, rstd = stats(x[rws].astype(F32))
                    xhat = centered * rstd
                    to = pl.ds(pl.multiple_of(i * T + rws.start, T), T)
                    xhat_ref[to] = xhat
                    act1[to] = (xhat * g1[...] + s1[...]).astype(BF)
                    act2[to] = (xhat * g2[...] + s2[...]).astype(BF)

                by_rows(T, T, norm)
            for c in c1:
                c.wait()
            for s, ref in enumerate((q, k, v)):
                wt = w1[:, :, :, s * QB : (s + 1) * QB].reshape(D, QB)

                def project(rws, s=s, ref=ref, wt=wt):
                    y = dot_nn(act1[rws], wt) + bq[:, s * QB : (s + 1) * QB]
                    for p in range(PAIRS):
                        z = y[:, p * 128 : (p + 1) * 128]
                        if s < 2:
                            z = z * cos[rws] + partner(z) * sin[rws]
                        ref[rws, p * 128 : (p + 1) * 128] = z.astype(BF)

                by_rows(NT, 256, project)

            def attend(i, carry):
                rws = pl.ds(pl.multiple_of(i * T, T), T)
                m2 = mask_ref[i]
                m2 = jnp.concatenate([m2, m2], axis=0)
                for p in range(PAIRS):
                    cols = slice(p * 128, (p + 1) * 128)
                    s = dot_nt(split_heads(q[rws, cols]), k[rws, cols]) * (1.0 / math.sqrt(HEAD)) + m2
                    e = jnp.exp(s - jnp.max(s, axis=-1, keepdims=True))
                    pr = e / jnp.sum(e, axis=-1, keepdims=True)
                    probs[i * PAIRS + p] = pr
                    pb = pr.astype(BF)
                    pb = jnp.concatenate([pb[:T], pb[T:]], axis=1)
                    mixed[rws, cols] = dot_nn(pb, split_heads(v[rws, cols])).astype(BF)
                return carry

            lax.fori_loop(0, NB, attend, 0)

            def feed(t, carry):
                cols = lanes(t, 256)
                wt = w1[:, :, :, pl.ds(pl.multiple_of(3 * QB + t * 256, 256), 256)].reshape(D, 256)

                def act(rws):
                    h = dot_nn(act2[rws], wt) + bi[:, cols]
                    cdf = 0.5 * (1.0 + lax.erf(h * (1.0 / math.sqrt(2.0))))
                    hidden[rws, cols] = (h * cdf).astype(BF)
                    dgelu[rws, cols] = cdf + h * (jnp.exp(-0.5 * h * h) * (1.0 / math.sqrt(2.0 * math.pi)))

                by_rows(NT, 256, act)
                return carry

            lax.fori_loop(0, FB // 256, feed, 0)
            for c in co + cout:
                c.wait()

            def project_out(t, carry):
                cols = lanes(t, 256)
                y = dot_nn(mixed[...], wo[:, :, cols].reshape(QB, 256))
                y = y + dot_nn(hidden[...], wout[:, :, cols].reshape(FB, 256))
                own[:, cols] = y[:T]
                for i, ref in enumerate((p1, p2, p3)):
                    ref[:, cols] = y[(i + 1) * T : (i + 2) * T].astype(BF)
                return carry

            lax.fori_loop(0, D // 256, project_out, 0)
            sends = [pltpu.make_async_copy(a, z, semp.at[i]) for i, (a, z) in enumerate(((p1, p1h), (p2, p2h), (p3, p3h)))]
            for c in sends:
                c.start()
            for c in sends:
                c.wait()

        tab = sds((NT, D), BF)
        third = sds((NT, QB), BF)
        block = sds((T, D), BF)
        act1, act2, q, k, v, probs, mixed, hidden, dgelu, xhat, full_one, full_o, full_out, own_part, *parts = call(
            fwd_body,
            [("s", br)] + [("v", x) for x in tokens]
            + [("v", a) for a in (cosine, sines, mask, bias_qkv, bias_in, gain_one, shift_one, gain_two, shift_two)]
            + [("a", a) for a in one + two],
            [tab, tab, third, third, third, sds((NB * PAIRS, 2 * T, T), F32), third, sds((NT, FB), BF), sds((NT, FB), F32),
             sds((NT, D), F32), sds((NB, R, rows, W1), BF), sds((R, rows, D), BF), sds((R, ff_dev, D), BF),
             sds((T, D), F32), block, block, block],
            [pltpu.VMEM((T, D), BF)] * 3 + [dma((R * NB,)), dma((R,)), dma((R,)), dma((3,))], hbm=(14, 15, 16),
            flops=2 * NT * D * W1 + 2 * NT * D * (QB + FB) + 8 * NT * T * QB,
        )

        returned = [shift(parts[k - 1], -k) for k in range(1, NB)]

        def total_body(x, live_ref, bo, own, p1, p2, p3, out):
            def fn(rws):
                y = x[rws].astype(F32) + bo[...] + own[rws]
                for ref in (p1, p2, p3):
                    y = y + ref[rws].astype(F32)
                out[rws] = (y * live_ref[rws]).astype(BF)

            by_rows(T, 32, fn)

        (block_out,) = call(
            total_body,
            [("v", a) for a in (block_in, live[:T], bias_o, own_part, *returned)], [block],
        )

        def bwd1_body(br, live_ref, g0, g1, g2, g3, act2, hidden, dgelu, wout, *rest):
            grad, dhid, keep, send, sum_in, term, flip = rest
            for i, g in enumerate((g0, g1, g2, g3)):

                def masked(rws, i=i, g=g):
                    to = pl.ds(pl.multiple_of(i * T + rws.start, T), T)
                    grad[to] = (g[rws].astype(F32) * live_ref[to]).astype(BF)

                by_rows(T, T, masked)

            def term_out(t, carry):
                flip[...] = hidden[:, lanes(t, 256)].T
                y = dot_nn(flip[...], grad[...])
                per = 256 // ff_dev
                term[pl.ds(t * per, per)] = y.reshape(per, ff_dev, D)
                return carry

            lax.fori_loop(0, FB // 256, term_out, 0)

            def to_out(j, carry):
                keep[j, MA:] = term[br[1] ^ (2 * j)]
                send[j, MA:] = term[br[1] ^ (2 * j + 1)].astype(BF)
                return carry

            lax.fori_loop(0, J, to_out, 0)

            def d_hidden(t, carry):
                cols = lanes(t, 256)
                per = 256 // ff_dev
                wt = wout[pl.ds(t * per, per)].reshape(256, D)
                y = (dot_nt(grad[...], wt) * dgelu[:, cols]).astype(BF)
                dhid[:, cols] = y
                sum_in[:, cols] = jnp.sum(y.astype(F32), axis=0, keepdims=True)
                return carry

            lax.fori_loop(0, FB // 256, d_hidden, 0)

            term_r = term.reshape(R * ff_dev // rows, rows, D) if ff_dev != rows else term

            def term_in(t, carry):
                flip[...] = act2[:, lanes(t, 256)].T
                term_r[:R] = dot_nn(flip[...], dhid[...]).reshape(R, rows, D)
                at = pl.ds(pl.multiple_of(t * rows, rows), rows)

                def one_j(j, carry):
                    keep[j, at] = term_r[br[1] ^ (2 * j)]
                    send[j, at] = term_r[br[1] ^ (2 * j + 1)].astype(BF)
                    return carry

                return lax.fori_loop(0, J, one_j, carry)

            lax.fori_loop(0, NB, term_in, 0)

        grad_r, dhid, keep_f, send_f, sum_in = call(
            bwd1_body,
            [("s", br), ("v", live)] + [("v", g) for g in grads_in] + [("v", a) for a in (act2, hidden, dgelu, full_out)],
            [tab, sds((NT, FB), BF), sds((J, MF, D), F32), sds((J, MF, D), BF), sds((1, FB), F32)],
            [pltpu.VMEM((R, ff_dev, D), F32), pltpu.VMEM((256, NT), BF)],
            flops=6 * NT * D * FB,
        )

        def bwd2_body(br, grad, mixed, act1, q, k, v, probs, cos, sin, wo, *rest):
            dqkv, keep, send, sum_qkv, dmix, term, term_o, flip = rest
            flip[...] = mixed[...].T
            term_o[...] = dot_nn(flip[...], grad[...]).reshape(R, rows, D)

            def to_o(j, carry):
                for c in range(NB):
                    cols = slice(c * QB, (c + 1) * QB)
                    keep[j, c * rows : (c + 1) * rows, 3 * QB :] = term_o[br[1] ^ (2 * j), :, cols]
                    send[j, c * rows : (c + 1) * rows, 3 * QB :] = term_o[br[1] ^ (2 * j + 1), :, cols].astype(BF)
                return carry

            lax.fori_loop(0, J, to_o, 0)
            dmix[...] = dot_nt(grad[...], wo[...].reshape(QB, D)).astype(BF)

            def attend(i, carry):
                rws = pl.ds(pl.multiple_of(i * T, T), T)
                for p in range(PAIRS):
                    cols = slice(p * 128, (p + 1) * 128)
                    pr = probs[i * PAIRS + p]
                    pb = pr.astype(BF)
                    dm2 = split_heads(dmix[rws, cols])
                    dp = dot_nt(dm2, v[rws, cols])
                    ds = (pr * (dp - jnp.sum(dp * pr, axis=-1, keepdims=True))).astype(BF)
                    dq = dot_nn(jnp.concatenate([ds[:T], ds[T:]], axis=1), split_heads(k[rws, cols]))
                    dk = dot_nn(ds.T, split_heads(q[rws, cols]))
                    dv = dot_nn(pb.T, dm2)
                    for s, z in enumerate((dq, dk)):
                        z = z * (1.0 / math.sqrt(HEAD))
                        z = z * cos[rws] - partner(z) * sin[rws]
                        dqkv[rws, s * QB + p * 128 : s * QB + (p + 1) * 128] = z.astype(BF)
                    dqkv[rws, 2 * QB + p * 128 : 2 * QB + (p + 1) * 128] = dv.astype(BF)
                return carry

            lax.fori_loop(0, NB, attend, 0)
            sum_qkv[...] = jnp.sum(dqkv[...].astype(F32), axis=0, keepdims=True)

            def term_qkv(t, carry):
                flip[...] = act1[:, lanes(t, 256)].T
                term[...] = dot_nn(flip[...], dqkv[...]).reshape(R, rows, 3 * QB)
                at = pl.ds(pl.multiple_of(t * rows, rows), rows)

                def one_j(j, carry):
                    keep[j, at, : 3 * QB] = term[br[1] ^ (2 * j)]
                    send[j, at, : 3 * QB] = term[br[1] ^ (2 * j + 1)].astype(BF)
                    return carry

                return lax.fori_loop(0, J, one_j, carry)

            lax.fori_loop(0, NB, term_qkv, 0)

        dqkv, keep_a, send_a, sum_qkv = call(
            bwd2_body,
            [("s", br)] + [("v", a) for a in (grad_r, mixed, act1, q, k, v, probs, cosine, sines, full_o)],
            [sds((NT, 3 * QB), BF), sds((J, MA, D), F32), sds((J, MA, D), BF), sds((1, 3 * QB), F32)],
            [pltpu.VMEM((NT, QB), BF), pltpu.VMEM((R, rows, 3 * QB), F32), pltpu.VMEM((R, rows, D), F32),
             pltpu.VMEM((256, NT), BF)],
            flops=2 * NT * D * (3 * QB + 2 * QB) + 16 * NT * T * QB,
        )

        def merge_body(keep, got, *outs):
            size = keep.shape[1]
            for j in range(J):

                def fn(rws, j=j):
                    y = keep[j, rws] + got[j, rws].astype(F32)
                    outs[j][rws] = y if j == 0 else y.astype(BF)

                by_rows(size, 32, fn)

        def merge(keep, send):
            size = keep.shape[1]
            got = swap(send, 1)
            outs = call(merge_body, [("v", keep), ("v", got)], [sds((size, D), F32)] + [sds((size, D), BF)] * (J - 1))
            return [outs[0]] + [swap(outs[j], 2 * j) for j in range(1, J)]

        merged_f = merge(keep_f, send_f)
        merged_a = merge(keep_a, send_a)

        out_widths = [FB * NB // n, 3 * D // n] + [D // n] * 5
        out_offsets = [sum(out_widths[:i]) for i in range(len(out_widths))]
        WO = -(-sum(out_widths) // 128) * 128

        def bwd3_body(br, xhat, w1, dqkv, dhid, grad, sum_in, sum_qkv, g1, g2, *rest):
            own, p1h, p2h, p3h, small, p1, p2, p3, gs, sums, semp = rest
            gs[...] = jnp.sum(grad[:T].astype(F32), axis=0, keepdims=True)

            def back(t, carry):
                cols = lanes(t, QB)
                d1 = dot_nt(dqkv[...], w1[t, :, :, : 3 * QB].reshape(QB, 3 * QB))
                d2 = dot_nt(dhid[...], w1[t, :, :, 3 * QB :].reshape(QB, FB))
                xh = xhat[:, cols]
                y = d1 * g1[:, cols] + d2 * g2[:, cols]
                own[:, cols] = y[:T]
                for i, ref in enumerate((p1, p2, p3)):
                    ref[:, cols] = y[(i + 1) * T : (i + 2) * T].astype(BF)
                for i, z in enumerate((d1 * xh, d1, d2 * xh, d2)):
                    sums[i : i + 1, cols] = jnp.sum(z, axis=0, keepdims=True)
                return carry

            lax.fori_loop(0, D // QB, back, 0)
            sends = [pltpu.make_async_copy(a, z, semp.at[i]) for i, (a, z) in enumerate(((p1, p1h), (p2, p2h), (p3, p3h)))]
            for c in sends:
                c.start()

            total = jnp.zeros((n, WO), F32)

            def place(total, vec, col, which):
                size = vec.shape[1]
                width, off = out_widths[which], out_offsets[which]
                mine = jnp.where(iota((n, size), 0) == lax.div(col, width), vec, 0.0)
                base = off // 128 * 128
                span = -(-(off + width) // 128) * 128 - base
                sel = pick(lax.rem(col, width), off, base, span)
                high = mine.astype(BF)
                low = (mine - high.astype(F32)).astype(BF)
                placed = dot_nt(high, sel) + dot_nt(low, sel)
                parts = []
                if base:
                    parts.append(jnp.zeros((n, base), F32))
                parts.append(placed)
                if base + span < WO:
                    parts.append(jnp.zeros((n, WO - base - span), F32))
                return total + (jnp.concatenate(parts, axis=1) if len(parts) > 1 else placed)

            whole = iota((1, D), 1)
            at = iota((1, 3 * QB), 1)
            total = place(total, sum_in[...], iota((1, FB), 1) + br[0] * FB, 0)
            total = place(total, sum_qkv[...], lax.div(at, QB) * D + br[0] * QB + lax.rem(at, QB), 1)
            total = place(total, gs[...], whole, 2)
            for i in range(4):
                total = place(total, sums[i : i + 1], whole, 3 + i)
            for i in range(8):
                small[:, i] = total[:, i * 128 : (i + 1) * 128] if (i + 1) * 128 <= WO else jnp.zeros((n, 128), F32)
            for c in sends:
                c.wait()

        own_g, g_1, g_2, g_3, small_grads = call(
            bwd3_body,
            [("s", br)] + [("v", a) for a in (xhat, full_one, dqkv, dhid, grad_r, sum_in, sum_qkv, gain_one, gain_two)],
            [sds((T, D), F32), block, block, block, sds((n, 8, 128), F32)],
            [pltpu.VMEM((T, D), BF)] * 3 + [pltpu.VMEM((1, D), F32), pltpu.VMEM((8, D), F32), dma((3,))], hbm=(1, 2, 3),
            flops=2 * NT * D * W1,
        )
        g_back = [shift(g, -k) for k, g in ((1, g_1), (2, g_2), (3, g_3))]
        small_back = lax.all_to_all(small_grads, "dp", 0, 0, tiled=True)

        def input_body(x, grad, own, p1, p2, p3, out):
            def fn(rws):
                centered, rstd = stats(x[rws].astype(F32))
                xh = centered * rstd
                g = own[rws]
                for ref in (p1, p2, p3):
                    g = g + ref[rws].astype(F32)
                mean_g = jnp.mean(g, axis=-1, keepdims=True)
                mean_gx = jnp.mean(g * xh, axis=-1, keepdims=True)
                out[rws] = (grad[rws].astype(F32) + rstd * (g - mean_g - xh * mean_gx)).astype(BF)

            by_rows(T, 32, fn)

        (grad_input,) = call(input_body, [("v", a) for a in (block_in, grad_r[:T], own_g, *g_back)], [block])

        def plane_f_body(br, *rest):
            got, (w_out_ref, z0, z1, z2, z3) = rest[:J], rest[J:]

            def out_rows(rws):
                y = got[0][pl.ds(pl.multiple_of(MA + rws.start, 8), rws.size)]
                for ref in got[1:]:
                    y = y + ref[pl.ds(pl.multiple_of(MA + rws.start, 8), rws.size)].astype(F32)
                w_out_ref[rws] = y

            by_rows(ff_dev, min(32, ff_dev), out_rows)
            for k, ref in enumerate((z0, z1, z2, z3)):
                at = pl.ds(pl.multiple_of(lax.rem(br[0] + k, NB) * rows, rows), rows)
                y = got[0][at]
                for other in got[1:]:
                    y = y + other[at].astype(F32)
                ref[...] = y if k == 0 else y.astype(BF)

        grad_w_out, zf0, *zf = call(
            plane_f_body, [("s", br)] + [("v", a) for a in merged_f],
            [sds((ff_dev, D), F32), sds((rows, FB), F32)] + [sds((rows, FB), BF)] * 3,
        )

        def plane_a_body(br, *rest):
            got, (w_o_ref, z0, z1, z2, z3) = rest[:J], rest[J:]
            for c in range(NB):
                y = got[0][c * rows : (c + 1) * rows, 3 * QB :]
                for other in got[1:]:
                    y = y + other[c * rows : (c + 1) * rows, 3 * QB :].astype(F32)
                w_o_ref[:, c * QB : (c + 1) * QB] = y
            for k, ref in enumerate((z0, z1, z2, z3)):
                at = pl.ds(pl.multiple_of(lax.rem(br[0] + k, NB) * rows, rows), rows)
                y = got[0][at, : 3 * QB]
                for other in got[1:]:
                    y = y + other[at, : 3 * QB].astype(F32)
                ref[...] = y if k == 0 else y.astype(BF)

        grad_w_o, za0, *za = call(
            plane_a_body, [("s", br)] + [("v", a) for a in merged_a],
            [sds((rows, D), F32), sds((rows, 3 * QB), F32)] + [sds((rows, 3 * QB), BF)] * 3,
        )
        zf = [zf0] + [shift(z, k + 1) for k, z in enumerate(zf)]
        za = [za0] + [shift(z, k + 1) for k, z in enumerate(za)]

        def place_f_body(br, z0, z1, z2, z3, out):
            for k, ref in enumerate((z0, z1, z2, z3)):
                out[:, lanes(lax.rem(br[0] + (NB - k), NB), FB)] = ref[...].astype(F32)

        def place_a_body(br, z0, z1, z2, z3, out):
            for k, ref in enumerate((z0, z1, z2, z3)):
                at = lax.rem(br[0] + (NB - k), NB)
                for s in range(3):
                    out[:, lanes(s * NB + at, QB)] = ref[:, s * QB : (s + 1) * QB].astype(F32)

        (grad_w_in,) = call(place_f_body, [("s", br)] + [("v", z) for z in zf], [sds((rows, NB * FB), F32)])
        (grad_w_qkv,) = call(place_a_body, [("s", br)] + [("v", z) for z in za], [sds((rows, 3 * D), F32)])

        summed = jnp.sum(small_back, axis=0).reshape(-1)
        outs = [summed[o : o + w] for o, w in zip(out_offsets, out_widths)]
        grad_b_in, grad_b_qkv, grad_b, grad_g1, grad_s1, grad_g2, grad_s2 = outs
        return (
            block_out, grad_input, grad_w_qkv, grad_b_qkv, grad_w_o, grad_b, grad_w_in, grad_b_in,
            grad_w_out, grad_b, grad_g1, grad_s1, grad_g2, grad_s2,
        )

    return on_device


def solution(mesh):
    two, one = P("dp", None), P("dp")
    n = mesh.shape["dp"]
    on_device = make(n)

    return jax.shard_map(
        on_device,
        mesh=mesh,
        in_specs=(two, two, two, one, two, one, two, one, two, one, one, one, one, one, P(), P(), P()),
        out_specs=(two, two, two, one, two, one, two, one, two, one, one, one, one, one),
        check_vma=False,
    )
```

```python
import math

import jax
import jax.numpy as jnp
from jax import lax
from jax.experimental import pallas as pl
from jax.experimental.pallas import tpu as pltpu
from jax.sharding import PartitionSpec as P


D = 1024
HEAD = 64
ROT = 16
NB = 4
QB = D // NB
NEG = -1e30

F32 = jnp.float32
BF = jnp.bfloat16
I32 = jnp.int32


def dot_nn(left, right):
    return jnp.dot(left, right, preferred_element_type=F32)


def dot_nt(left, right):
    return lax.dot_general(left, right, (((1,), (1,)), ((), ())), preferred_element_type=F32)


def iota(shape, axis):
    return lax.broadcasted_iota(I32, shape, axis)


def call(body, ins, outs, scratch=(), flops=0, extra=4 << 20, hbm=(), alias=None):
    spaces = {"v": pltpu.VMEM, "s": pltpu.SMEM, "a": pl.ANY}
    arrays = [a for _, a in ins]
    nbytes = sum(a.size * a.dtype.itemsize for a in arrays) + sum(math.prod(o.shape) * o.dtype.itemsize for o in outs)
    room = sum(math.prod(t.shape) * jnp.dtype(t.dtype).itemsize for t in scratch if getattr(t, "memory_space", None) == pltpu.VMEM)
    room += sum(a.size * a.dtype.itemsize for s, a in ins if s == "v") + sum(math.prod(o.shape) * o.dtype.itemsize for i, o in enumerate(outs) if i not in hbm)
    return pl.pallas_call(
        body,
        out_shape=tuple(outs),
        in_specs=[pl.BlockSpec(memory_space=spaces[s]) for s, _ in ins],
        out_specs=tuple(pl.BlockSpec(memory_space=pltpu.HBM if i in hbm else pltpu.VMEM) for i in range(len(outs))),
        scratch_shapes=list(scratch),
        input_output_aliases=alias or {},
        compiler_params=pltpu.CompilerParams(vmem_limit_bytes=int(room * 1.02) + extra),
        cost_estimate=pl.CostEstimate(flops=int(flops), bytes_accessed=int(nbytes), transcendentals=0),
    )(*arrays)


def sds(shape, dtype):
    return jax.ShapeDtypeStruct(shape, dtype)


def by_rows(count, chunk, fn):
    def step(i, carry):
        fn(pl.ds(pl.multiple_of(i * chunk, chunk), chunk))
        return carry

    lax.fori_loop(0, count // chunk, step, 0)


def lanes(i, width):
    return pl.ds(pl.multiple_of(i * width, width), width)


def partner(v):
    low = iota(v.shape, 1) % HEAD < ROT // 2
    return jnp.where(low, pltpu.roll(v, v.shape[1] - ROT // 2, 1), pltpu.roll(v, ROT // 2, 1))


def split_heads(v):
    first = iota(v.shape, 1) < HEAD
    zero = jnp.zeros_like(v)
    return jnp.concatenate([jnp.where(first, v, zero), jnp.where(first, zero, v)], axis=0)


def stats(x):
    centre = jnp.mean(x, axis=-1, keepdims=True)
    centered = x - centre
    spread = jnp.mean(centered * centered, axis=-1, keepdims=True)
    return centered, lax.rsqrt(spread + 1e-05)


def make(n):
    R = n // NB
    assert R * NB == n and R & (R - 1) == 0

    def across(v, mask):
        return lax.ppermute(v, "dp", [(d, d ^ (mask * R)) for d in range(n)])

    def swap(v, mask):
        return lax.ppermute(v, "dp", [(d, d ^ mask) for d in range(n)])

    def gather_r(own):
        half = own.shape[0] // 2
        got = [(0, 0, own)]
        if R == 8:
            from_x, from_y = swap(own, 2), swap(own, 4)
            got += [(2, 0, from_x), (4, 0, from_y)]
            got.append((6, 0, swap(from_y[:half], 2)))
            got.append((6, half, swap(from_x[half:], 4)))
        else:
            for m in range(2, R, 2):
                got.append((m, 0, swap(own, m)))
        return got + [(m + 1, at, swap(v, 1)) for m, at, v in got]

    def on_device(
        block_in, grad_out, w_qkv, b_qkv, w_o, b_o, w_in, b_in, w_out, b_out,
        ln1_gain, ln1_shift, ln2_gain, ln2_shift, seq_lens, seq_device, seq_offset,
    ):
        T = block_in.shape[0]
        NT = NB * T
        rows = w_qkv.shape[0]
        ff_dev = w_out.shape[0]
        FB = w_in.shape[1] // NB
        W1 = 3 * QB + FB
        J = R // 2
        MF = NB * rows + ff_dev
        MA = NB * rows
        MS = MA + 8
        idx = lax.axis_index("dp").astype(I32)
        b, r = idx // R, idx % R
        br = jnp.stack([b, r])

        slots1 = jnp.arange(T, dtype=I32)
        owners = [(b ^ k) * R + r for k in range(NB)]
        device = jnp.concatenate([jnp.full((T,), o, I32) for o in owners])
        slots = jnp.tile(slots1, NB)
        count = seq_lens.shape[0]
        inside = (
            (seq_device[None, :] == device[:, None])
            & (slots[:, None] >= seq_offset[None, :])
            & (slots[:, None] < (seq_offset + seq_lens)[None, :])
        )
        number = jnp.arange(count, dtype=I32)
        present = jnp.any(inside, axis=1)
        segment = jnp.where(present, jnp.sum(jnp.where(inside, number[None, :], 0), axis=1), count + slots)
        position = jnp.sum(jnp.where(inside, slots[:, None] - seq_offset[None, :], 0), axis=1)
        live = present.astype(F32)[:, None]
        seg = segment.reshape(NB, T)
        allowed = (seg[:, :, None] == seg[:, None, :]) & (slots1[None, None, :] <= slots1[None, :, None])
        mask = jnp.where(allowed, 0.0, NEG).astype(F32)
        lane = jnp.arange(2 * HEAD, dtype=I32) % HEAD
        half = ROT // 2
        freqs = 10000.0 ** (-(lane % half).astype(F32) / half)
        angle = position.astype(F32)[:, None] * jnp.where(lane < ROT, freqs, 0.0)[None, :]
        cosine = jnp.cos(angle)
        sines = jnp.sin(angle) * jnp.where(lane < half, -1.0, 1.0)[None, :]

        small = [b_in, b_qkv, b_o, b_out, ln1_gain, ln1_shift, ln2_gain, ln2_shift]
        widths = [v.shape[0] for v in small]
        offsets = [sum(widths[:i]) for i in range(len(small))]
        WS = 1024

        def pack_body(br, qkv_ref, in_ref, o_ref, out_ref, *rest):
            vectors, outs = rest[: len(small)], rest[len(small) :]
            for k in range(NB):
                to = br[0] ^ k
                for s in range(3):
                    outs[k][:, s * QB : (s + 1) * QB] = qkv_ref[:, lanes(s * NB + to, QB)]
                outs[k][:, 3 * QB :] = in_ref[:, lanes(to, FB)]
            outs[NB][:ff_dev] = out_ref[...]
            outs[NB][ff_dev:] = o_ref[...]
            parts = [v[...].astype(F32) for v in vectors]
            if WS > sum(widths):
                parts.append(jnp.zeros((1, WS - sum(widths)), F32))
            every = jnp.concatenate(parts, axis=1)
            for i in range(8):
                outs[NB + 1][:, i] = jnp.broadcast_to(every[:, i * 128 : (i + 1) * 128], (n, 128)).astype(BF)

        packed = call(
            pack_body,
            [("s", br), ("v", w_qkv), ("v", w_in), ("v", w_o), ("v", w_out)] + [("v", v.reshape(1, -1)) for v in small],
            [sds((rows, W1), BF)] * NB + [sds((ff_dev + rows, D), BF), sds((n, 8, 128), BF)], extra=56 << 20,
        )
        columns, own_two, small_out = packed[:NB], packed[NB], packed[NB + 1]

        def blocks_of(own, after):
            two = across(after, 2)
            return [own, across(after, 1), two, across(two, 1)]

        mine = jnp.concatenate([columns[0]] + [across(columns[k], k) for k in range(1, NB)]).reshape(NB, rows, W1)
        two = gather_r(own_two)
        one = gather_r(mine)
        after, _ = lax.optimization_barrier((block_in, mine))
        tokens = blocks_of(block_in, after)
        small_in = lax.all_to_all(small_out, "dp", 0, 0, tiled=True)
        after, _ = lax.optimization_barrier((grad_out, tokens[1]))
        grads_in = blocks_of(grad_out, after)

        def pick(width_mod, off, base, width):
            return (iota((width, width_mod.shape[1]), 0) + base == off + width_mod).astype(BF)

        def window(off, width):
            base = off // 128 * 128
            return base, -(-(off + width) // 128) * 128 - base

        def dec_body(br, got, bq, bi, g1, s1, g2, s2, bo):
            def expand(which, col):
                width, off = widths[which], offsets[which]
                base, span = window(off, width)
                total = col.shape[1]
                sel = pick(lax.rem(col, width), off, base, span)
                every = dot_nn(jnp.concatenate([got[:, i] for i in range(base // 128, (base + span) // 128)], axis=1), sel)
                return jnp.sum(jnp.where(iota((n, total), 0) == lax.div(col, width), every, 0.0), axis=0, keepdims=True)

            at = iota((1, 3 * QB), 1)
            bq[...] = expand(1, lax.div(at, QB) * D + br[0] * QB + lax.rem(at, QB))
            bi[...] = expand(0, iota((1, FB), 1) + br[0] * FB)
            whole = iota((1, D), 1)
            bo[...] = expand(2, whole) + expand(3, whole)
            for ref, which in ((g1, 4), (s1, 5), (g2, 6), (s2, 7)):
                ref[...] = expand(which, whole)

        row = sds((1, D), F32)
        bias_qkv, bias_in, gain_one, shift_one, gain_two, shift_two, bias_o = call(
            dec_body, [("s", br), ("v", small_in)], [sds((1, 3 * QB), F32), sds((1, FB), F32)] + [row] * 5
        )

        def load_one(br, parts, w1, sems):
            copies = []
            for (m, start, _), ref in zip(one, parts):
                for k in range(ref.shape[0]):
                    sem = sems.at[len(copies)]
                    copies.append(pltpu.make_async_copy(ref.at[k], w1.at[br[0] ^ (start + k), br[1] ^ m], sem))
            return copies

        def load_two(br, parts, wout, wo, sems):
            copies = []
            for (m, start, _), ref in zip(two, parts):
                size = ref.shape[0]
                for to, first, last in ((wout, 0, ff_dev), (wo, ff_dev, ff_dev + rows)):
                    low, high = max(start, first), min(start + size, last)
                    if low < high:
                        copies.append(
                            pltpu.make_async_copy(
                                ref.at[pl.ds(low - start, high - low)],
                                to.at[br[1] ^ m, pl.ds(low - first, high - low)],
                                sems.at[len(copies)],
                            )
                        )
            return copies

        dma = pltpu.SemaphoreType.DMA
        PAIRS = QB // 128

        def fwd_body(br, x0, x1, x2, x3, cos, sin, mask_ref, bq, bi, g1, s1, g2, s2, *rest):
            one_refs, two_refs, rest = rest[: len(one)], rest[len(one) : len(one) + len(two)], rest[len(one) + len(two) :]
            act1, act2, q, k, v, probs, mixed, hidden, dgelu, xhat_ref, w1, wo, wout, own, later, away = rest[:16]
            stage, sem1, sem2, semp = rest[16:]
            c1, c2 = load_one(br, one_refs, w1, sem1), load_two(br, two_refs, wout, wo, sem2)
            for c in c1 + c2:
                c.start()
            for i, x in enumerate((x0, x1, x2, x3)):

                def norm(rws, i=i, x=x):
                    centered, rstd = stats(x[rws].astype(F32))
                    xhat = centered * rstd
                    to = pl.ds(pl.multiple_of(i * T + rws.start, T), T)
                    xhat_ref[to] = xhat
                    act1[to] = (xhat * g1[...] + s1[...]).astype(BF)
                    act2[to] = (xhat * g2[...] + s2[...]).astype(BF)

                by_rows(T, T, norm)
            for c in c1:
                c.wait()
            for s, ref in enumerate((q, k, v)):
                wt = w1[:, :, :, s * QB : (s + 1) * QB].reshape(D, QB)

                def project(rws, s=s, ref=ref, wt=wt):
                    y = dot_nn(act1[rws], wt) + bq[:, s * QB : (s + 1) * QB]
                    for p in range(PAIRS):
                        z = y[:, p * 128 : (p + 1) * 128]
                        if s < 2:
                            z = z * cos[rws] + partner(z) * sin[rws]
                        ref[rws, p * 128 : (p + 1) * 128] = z.astype(BF)

                by_rows(NT, 256, project)

            def attend(i, carry):
                rws = pl.ds(pl.multiple_of(i * T, T), T)
                m2 = mask_ref[i]
                m2 = jnp.concatenate([m2, m2], axis=0)
                for p in range(PAIRS):
                    cols = slice(p * 128, (p + 1) * 128)
                    s = dot_nt(split_heads(q[rws, cols]), k[rws, cols]) * (1.0 / math.sqrt(HEAD)) + m2
                    e = jnp.exp(s - jnp.max(s, axis=-1, keepdims=True))
                    pr = e / jnp.sum(e, axis=-1, keepdims=True)
                    probs[i * PAIRS + p] = pr
                    pb = pr.astype(BF)
                    pb = jnp.concatenate([pb[:T], pb[T:]], axis=1)
                    mixed[rws, cols] = dot_nn(pb, split_heads(v[rws, cols])).astype(BF)
                return carry

            lax.fori_loop(0, NB, attend, 0)

            def feed(t, carry):
                cols = lanes(t, 256)
                wt = w1[:, :, :, pl.ds(pl.multiple_of(3 * QB + t * 256, 256), 256)].reshape(D, 256)

                def act(rws):
                    h = dot_nn(act2[rws], wt) + bi[:, cols]
                    cdf = 0.5 * (1.0 + lax.erf(h * (1.0 / math.sqrt(2.0))))
                    hidden[rws, cols] = (h * cdf).astype(BF)
                    dgelu[rws, cols] = cdf + h * (jnp.exp(-0.5 * h * h) * (1.0 / math.sqrt(2.0 * math.pi)))

                by_rows(NT, 256, act)
                return carry

            lax.fori_loop(0, FB // 256, feed, 0)
            for c in c2:
                c.wait()

            def project_out(t, carry):
                cols = lanes(t, 256)
                y = dot_nn(mixed[...], wo[:, :, cols].reshape(QB, 256))
                y = y + dot_nn(hidden[...], wout[:, :, cols].reshape(FB, 256))
                own[:, cols] = y[:T]
                later[:, cols] = y[2 * T : 3 * T]
                stage[:T, cols] = y[T : 2 * T].astype(BF)
                stage[T:, cols] = y[3 * T :].astype(BF)
                return carry

            lax.fori_loop(0, D // 256, project_out, 0)
            send = pltpu.make_async_copy(stage, away, semp)
            send.start()
            send.wait()

        tab = sds((NT, D), BF)
        third = sds((NT, QB), BF)
        block = sds((T, D), BF)
        act1, act2, q, k, v, probs, mixed, hidden, dgelu, xhat, full_one, full_o, full_out, own_part, later_part, away_part = call(
            fwd_body,
            [("s", br)] + [("v", x) for x in tokens]
            + [("v", a) for a in (cosine, sines, mask, bias_qkv, bias_in, gain_one, shift_one, gain_two, shift_two)]
            + [("a", a) for _, _, a in one + two],
            [tab, tab, third, third, third, sds((NB * PAIRS, 2 * T, T), F32), third, sds((NT, FB), BF), sds((NT, FB), F32),
             sds((NT, D), F32), sds((NB, R, rows, W1), BF), sds((R, rows, D), BF), sds((R, ff_dev, D), BF),
             sds((T, D), F32), sds((T, D), F32), sds((2 * T, D), BF)],
            [pltpu.VMEM((2 * T, D), BF), dma((R * NB,)), dma((3 * R,)), dma], hbm=(15,),
            flops=2 * NT * D * W1 + 2 * NT * D * (QB + FB) + 8 * NT * T * QB,
        )

        got_one = across(away_part, 1)

        def pass_body(keep, got, out):
            def fn(rws):
                out[rws] = (keep[rws] + got[pl.ds(T, T)].astype(F32)).astype(BF)

            by_rows(T, T, fn)

        (pass_part,) = call(pass_body, [("v", later_part), ("v", got_one)], [block])
        got_two = across(pass_part, 2)

        def total_body(x, live_ref, bo, own, p1, p2, out):
            def fn(rws):
                y = x[rws].astype(F32) + bo[...] + own[rws] + p1[rws].astype(F32) + p2[rws].astype(F32)
                out[rws] = (y * live_ref[rws]).astype(BF)

            by_rows(T, T, fn)

        (block_out,) = call(
            total_body,
            [("v", a) for a in (block_in, live[:T], bias_o, own_part, got_one, got_two)], [block],
        )

        def bwd1_body(br, live_ref, g0, g1, g2, g3, act2, hidden, dgelu, wout, *rest):
            grad, dhid, keep, send, sum_in, term, flip = rest
            for i, g in enumerate((g0, g1, g2, g3)):

                def masked(rws, i=i, g=g):
                    to = pl.ds(pl.multiple_of(i * T + rws.start, T), T)
                    grad[to] = (g[rws].astype(F32) * live_ref[to]).astype(BF)

                by_rows(T, T, masked)

            def term_out(t, carry):
                flip[...] = hidden[:, lanes(t, 256)].T
                y = dot_nn(flip[...], grad[...])
                per = 256 // ff_dev
                term[pl.ds(t * per, per)] = y.reshape(per, ff_dev, D)
                return carry

            lax.fori_loop(0, FB // 256, term_out, 0)

            def to_out(j, carry):
                keep[j, MA:] = term[br[1] ^ (2 * j)]
                send[j, MA:] = term[br[1] ^ (2 * j + 1)].astype(BF)
                return carry

            lax.fori_loop(0, J, to_out, 0)

            def d_hidden(t, carry):
                cols = lanes(t, 256)
                per = 256 // ff_dev
                wt = wout[pl.ds(t * per, per)].reshape(256, D)
                y = (dot_nt(grad[...], wt) * dgelu[:, cols]).astype(BF)
                dhid[:, cols] = y
                sum_in[:, cols] = jnp.sum(y.astype(F32), axis=0, keepdims=True)
                return carry

            lax.fori_loop(0, FB // 256, d_hidden, 0)

            term_r = term.reshape(R * ff_dev // rows, rows, D) if ff_dev != rows else term

            def term_in(t, carry):
                flip[...] = act2[:, lanes(t, 256)].T
                term_r[:R] = dot_nn(flip[...], dhid[...]).reshape(R, rows, D)
                at = pl.ds(pl.multiple_of(t * rows, rows), rows)

                def one_j(j, carry):
                    keep[j, at] = term_r[br[1] ^ (2 * j)]
                    send[j, at] = term_r[br[1] ^ (2 * j + 1)].astype(BF)
                    return carry

                return lax.fori_loop(0, J, one_j, carry)

            lax.fori_loop(0, NB, term_in, 0)

        grad_r, dhid, keep_f, send_f, sum_in = call(
            bwd1_body,
            [("s", br), ("v", live)] + [("v", g) for g in grads_in] + [("v", a) for a in (act2, hidden, dgelu, full_out)],
            [tab, sds((NT, FB), BF), sds((J, MF, D), F32), sds((J, MF, D), BF), sds((1, FB), F32)],
            [pltpu.VMEM((R, ff_dev, D), F32), pltpu.VMEM((256, NT), BF)],
            flops=6 * NT * D * FB,
        )

        def bwd2_body(br, grad, mixed, act1, q, k, v, probs, cos, sin, wo, *rest):
            dqkv, keep, send, sum_qkv, dmix, term, term_o, flip = rest
            flip[...] = mixed[...].T
            term_o[...] = dot_nn(flip[...], grad[...]).reshape(R, rows, D)

            def to_o(j, carry):
                for c in range(NB):
                    cols = slice(c * QB, (c + 1) * QB)
                    keep[j, c * rows : (c + 1) * rows, 3 * QB :] = term_o[br[1] ^ (2 * j), :, cols]
                    send[j, c * rows : (c + 1) * rows, 3 * QB :] = term_o[br[1] ^ (2 * j + 1), :, cols].astype(BF)
                return carry

            lax.fori_loop(0, J, to_o, 0)
            dmix[...] = dot_nt(grad[...], wo[...].reshape(QB, D)).astype(BF)

            def attend(i, carry):
                rws = pl.ds(pl.multiple_of(i * T, T), T)
                for p in range(PAIRS):
                    cols = slice(p * 128, (p + 1) * 128)
                    pr = probs[i * PAIRS + p]
                    pb = pr.astype(BF)
                    dm2 = split_heads(dmix[rws, cols])
                    dp = dot_nt(dm2, v[rws, cols])
                    ds = (pr * (dp - jnp.sum(dp * pr, axis=-1, keepdims=True))).astype(BF)
                    dq = dot_nn(jnp.concatenate([ds[:T], ds[T:]], axis=1), split_heads(k[rws, cols]))
                    dk = dot_nn(ds.T, split_heads(q[rws, cols]))
                    dv = dot_nn(pb.T, dm2)
                    for s, z in enumerate((dq, dk)):
                        z = z * (1.0 / math.sqrt(HEAD))
                        z = z * cos[rws] - partner(z) * sin[rws]
                        dqkv[rws, s * QB + p * 128 : s * QB + (p + 1) * 128] = z.astype(BF)
                    dqkv[rws, 2 * QB + p * 128 : 2 * QB + (p + 1) * 128] = dv.astype(BF)
                return carry

            lax.fori_loop(0, NB, attend, 0)
            sum_qkv[...] = jnp.sum(dqkv[...].astype(F32), axis=0, keepdims=True)

            def term_qkv(t, carry):
                flip[...] = act1[:, lanes(t, 256)].T
                term[...] = dot_nn(flip[...], dqkv[...]).reshape(R, rows, 3 * QB)
                at = pl.ds(pl.multiple_of(t * rows, rows), rows)

                def one_j(j, carry):
                    keep[j, at, : 3 * QB] = term[br[1] ^ (2 * j)]
                    send[j, at, : 3 * QB] = term[br[1] ^ (2 * j + 1)].astype(BF)
                    return carry

                return lax.fori_loop(0, J, one_j, carry)

            lax.fori_loop(0, NB, term_qkv, 0)

        dqkv, keep_a, send_a, sum_qkv = call(
            bwd2_body,
            [("s", br)] + [("v", a) for a in (grad_r, mixed, act1, q, k, v, probs, cosine, sines, full_o)],
            [sds((NT, 3 * QB), BF), sds((J, MS, D), F32), sds((J, MS, D), BF), sds((1, 3 * QB), F32)],
            [pltpu.VMEM((NT, QB), BF), pltpu.VMEM((R, rows, 3 * QB), F32), pltpu.VMEM((R, rows, D), F32),
             pltpu.VMEM((256, NT), BF)],
            flops=2 * NT * D * (3 * QB + 2 * QB) + 16 * NT * T * QB,
        )

        def merge_body(keep, got, *outs):
            size = keep.shape[1]
            for j in range(J):

                def fn(rws, j=j):
                    y = keep[j, rws] + got[j, rws].astype(F32)
                    outs[j][rws] = y if j == 0 else y.astype(BF)

                by_rows(size, size, fn)

        def merge(keep, send):
            size = keep.shape[1]
            got = swap(send, 1)
            outs = call(merge_body, [("v", keep), ("v", got)], [sds((size, D), F32)] + [sds((size, D), BF)] * (J - 1))
            return [outs[0]] + [swap(outs[j], 2 * j) for j in range(1, J)]

        merged_f = merge(keep_f, send_f)
        out_widths = [FB * NB // n, 3 * D // n] + [D // n] * 5
        out_offsets = [sum(out_widths[:i]) for i in range(len(out_widths))]
        WO = -(-sum(out_widths) // 128) * 128

        def bwd3_body(br, xhat, w1, dqkv, dhid, grad, sum_in, sum_qkv, g1, g2, keep_in, send_in, *rest):
            own, p1h, p2h, p3h, keep, send, p1, p2, p3, gs, sums, tot, semp = rest
            gs[...] = jnp.sum(grad[:T].astype(F32), axis=0, keepdims=True)

            def back(t, carry):
                cols = lanes(t, QB)
                d1 = dot_nt(dqkv[...], w1[t, :, :, : 3 * QB].reshape(QB, 3 * QB))
                d2 = dot_nt(dhid[...], w1[t, :, :, 3 * QB :].reshape(QB, FB))
                xh = xhat[:, cols]
                y = d1 * g1[:, cols] + d2 * g2[:, cols]
                own[:, cols] = y[:T]
                for i, ref in enumerate((p1, p2, p3)):
                    ref[:, cols] = y[(i + 1) * T : (i + 2) * T].astype(BF)
                for i, z in enumerate((d1 * xh, d1, d2 * xh, d2)):
                    sums[i : i + 1, cols] = jnp.sum(z, axis=0, keepdims=True)
                return carry

            lax.fori_loop(0, D // QB, back, 0)
            sends = [pltpu.make_async_copy(a, z, semp.at[i]) for i, (a, z) in enumerate(((p1, p1h), (p2, p2h), (p3, p3h)))]
            for c in sends:
                c.start()

            total = jnp.zeros((n, WO), F32)

            def place(total, vec, col, which):
                size = vec.shape[1]
                width, off = out_widths[which], out_offsets[which]
                mine = jnp.where(iota((n, size), 0) == lax.div(col, width), vec, 0.0)
                base = off // 128 * 128
                span = -(-(off + width) // 128) * 128 - base
                sel = pick(lax.rem(col, width), off, base, span)
                high = mine.astype(BF)
                low = (mine - high.astype(F32)).astype(BF)
                placed = dot_nt(high, sel) + dot_nt(low, sel)
                parts = []
                if base:
                    parts.append(jnp.zeros((n, base), F32))
                parts.append(placed)
                if base + span < WO:
                    parts.append(jnp.zeros((n, WO - base - span), F32))
                return total + (jnp.concatenate(parts, axis=1) if len(parts) > 1 else placed)

            whole = iota((1, D), 1)
            at = iota((1, 3 * QB), 1)
            total = place(total, sum_in[...], iota((1, FB), 1) + br[0] * FB, 0)
            total = place(total, sum_qkv[...], lax.div(at, QB) * D + br[0] * QB + lax.rem(at, QB), 1)
            total = place(total, gs[...], whole, 2)
            for i in range(4):
                total = place(total, sums[i : i + 1], whole, 3 + i)
            tot[...] = total
            for j in range(J):
                for ref, m in ((keep, 2 * j), (send, 2 * j + 1)):
                    lines = [tot[pl.ds(to * R + (br[1] ^ m), 1), :] for to in range(NB)]
                    lines.append(jnp.zeros((MS - MA - NB, WO), F32))
                    ref[j, MA:, :WO] = jnp.concatenate(lines, axis=0).astype(ref.dtype)
            for c in sends:
                c.wait()

        own_g, g_1, g_2, g_3, keep_a, send_a = call(
            bwd3_body,
            [("s", br)] + [("v", a) for a in (xhat, full_one, dqkv, dhid, grad_r, sum_in, sum_qkv, gain_one, gain_two, keep_a, send_a)],
            [sds((T, D), F32), block, block, block, sds((J, MS, D), F32), sds((J, MS, D), BF)],
            [pltpu.VMEM((T, D), BF)] * 3 + [pltpu.VMEM((1, D), F32), pltpu.VMEM((8, D), F32), pltpu.VMEM((n, WO), F32), dma((3,))], hbm=(1, 2, 3),
            alias={10: 4, 11: 5},
            flops=2 * NT * D * W1,
        )
        g_back = [across(g, k) for k, g in ((1, g_1), (2, g_2), (3, g_3))]
        merged_a = merge(keep_a, send_a)

        def input_body(x, grad, own, p1, p2, p3, out):
            def fn(rws):
                centered, rstd = stats(x[rws].astype(F32))
                xh = centered * rstd
                g = own[rws]
                for ref in (p1, p2, p3):
                    g = g + ref[rws].astype(F32)
                mean_g = jnp.mean(g, axis=-1, keepdims=True)
                mean_gx = jnp.mean(g * xh, axis=-1, keepdims=True)
                out[rws] = (grad[rws].astype(F32) + rstd * (g - mean_g - xh * mean_gx)).astype(BF)

            by_rows(T, T, fn)

        (grad_input,) = call(input_body, [("v", a) for a in (block_in, grad_r[:T], own_g, *g_back)], [block])

        def plane_f_body(br, *rest):
            got, (w_out_ref, z0, z1, z2, z3) = rest[:J], rest[J:]

            def out_rows(rws):
                y = got[0][pl.ds(pl.multiple_of(MA + rws.start, 8), rws.size)]
                for ref in got[1:]:
                    y = y + ref[pl.ds(pl.multiple_of(MA + rws.start, 8), rws.size)].astype(F32)
                w_out_ref[rws] = y

            by_rows(ff_dev, min(32, ff_dev), out_rows)
            for k, ref in enumerate((z0, z1, z2, z3)):
                at = pl.ds(pl.multiple_of((br[0] ^ k) * rows, rows), rows)
                y = got[0][at]
                for other in got[1:]:
                    y = y + other[at].astype(F32)
                ref[...] = y if k == 0 else y.astype(BF)

        grad_w_out, zf0, *zf = call(
            plane_f_body, [("s", br)] + [("v", a) for a in merged_f],
            [sds((ff_dev, D), F32), sds((rows, FB), F32)] + [sds((rows, FB), BF)] * 3,
        )

        def plane_a_body(br, *rest):
            got, (w_o_ref, z0, z1, z2, z3) = rest[:J], rest[J:]
            for c in range(NB):
                y = got[0][c * rows : (c + 1) * rows, 3 * QB :]
                for other in got[1:]:
                    y = y + other[c * rows : (c + 1) * rows, 3 * QB :].astype(F32)
                w_o_ref[:, c * QB : (c + 1) * QB] = y
            for k, ref in enumerate((z0, z1, z2, z3)):
                at = pl.ds(pl.multiple_of((br[0] ^ k) * rows, rows), rows)
                y = got[0][at, : 3 * QB]
                for other in got[1:]:
                    y = y + other[at, : 3 * QB].astype(F32)
                ref[:rows] = y if k == 0 else y.astype(BF)
                y = got[0][MA:, :WO]
                for other in got[1:]:
                    y = y + other[MA:, :WO].astype(F32)
                y = jnp.sum(jnp.where(iota(y.shape, 0) == (br[0] ^ k), y, 0.0), axis=0, keepdims=True)
                ref[rows:, :WO] = jnp.broadcast_to(y, (8, WO)).astype(ref.dtype)

        grad_w_o, za0, *za = call(
            plane_a_body, [("s", br)] + [("v", a) for a in merged_a],
            [sds((rows, D), F32), sds((rows + 8, 3 * QB), F32)] + [sds((rows + 8, 3 * QB), BF)] * 3,
        )
        zf = [zf0] + [across(z, k + 1) for k, z in enumerate(zf)]
        za = [za0] + [across(z, k + 1) for k, z in enumerate(za)]

        def place_f_body(br, z0, z1, z2, z3, out):
            for k, ref in enumerate((z0, z1, z2, z3)):
                out[:, lanes(br[0] ^ k, FB)] = ref[...].astype(F32)

        def place_a_body(br, z0, z1, z2, z3, out, *small):
            y = sum(ref[rows:, :WO].astype(F32) for ref in (z0, z1, z2, z3))
            for ref, at, width in zip(small, out_offsets, out_widths):
                ref[...] = y[:1, at : at + width]
            for k, ref in enumerate((z0, z1, z2, z3)):
                at = br[0] ^ k
                for s in range(3):
                    out[:, lanes(s * NB + at, QB)] = ref[:rows, s * QB : (s + 1) * QB].astype(F32)

        (grad_w_in,) = call(place_f_body, [("s", br)] + [("v", z) for z in zf], [sds((rows, NB * FB), F32)])
        grad_w_qkv, *outs = call(
            place_a_body, [("s", br)] + [("v", z) for z in za],
            [sds((rows, 3 * D), F32)] + [sds((1, w), F32) for w in out_widths],
        )
        outs = [o.reshape(-1) for o in outs]

        grad_b_in, grad_b_qkv, grad_b, grad_g1, grad_s1, grad_g2, grad_s2 = outs
        return (
            block_out, grad_input, grad_w_qkv, grad_b_qkv, grad_w_o, grad_b, grad_w_in, grad_b_in,
            grad_w_out, grad_b, grad_g1, grad_s1, grad_g2, grad_s2,
        )

    return on_device


def solution(mesh):
    two, one = P("dp", None), P("dp")
    n = mesh.shape["dp"]
    on_device = make(n)

    return jax.shard_map(
        on_device,
        mesh=mesh,
        in_specs=(two, two, two, one, two, one, two, one, two, one, one, one, one, one, P(), P(), P()),
        out_specs=(two, two, two, one, two, one, two, one, two, one, one, one, one, one),
        check_vma=False,
    )
```

```python
import functools
import math

import jax
import jax.numpy as jnp
from jax import lax
from jax.experimental import pallas as pl
from jax.experimental.pallas import tpu as pltpu
from jax.sharding import PartitionSpec as P


D = 1024
HEAD = 64
ROT = 16
NB = 4
QB = D // NB
NEG = -1e30
SHARE = 1.0

F32 = jnp.float32
BF = jnp.bfloat16
I32 = jnp.int32


def dot_nn(left, right):
    return jnp.dot(left, right, preferred_element_type=F32)


def dot_nt(left, right):
    return lax.dot_general(left, right, (((1,), (1,)), ((), ())), preferred_element_type=F32)


def iota(shape, axis):
    return lax.broadcasted_iota(I32, shape, axis)


def call(body, ins, outs, scratch=(), flops=0, extra=4 << 20, hbm=(), alias=None):
    spaces = {"v": pltpu.VMEM, "s": pltpu.SMEM, "a": pl.ANY, "h": pltpu.HBM}
    arrays = [a for _, a in ins]
    nbytes = sum(a.size * a.dtype.itemsize for a in arrays) + sum(math.prod(o.shape) * o.dtype.itemsize for o in outs)
    room = sum(math.prod(t.shape) * jnp.dtype(t.dtype).itemsize for t in scratch if getattr(t, "memory_space", None) == pltpu.VMEM)
    room += SHARE * (sum(a.size * a.dtype.itemsize for s, a in ins if s == "v") + sum(math.prod(o.shape) * o.dtype.itemsize for i, o in enumerate(outs) if i not in hbm))
    return pl.pallas_call(
        body,
        out_shape=tuple(outs),
        in_specs=[pl.BlockSpec(memory_space=spaces[s]) for s, _ in ins],
        out_specs=tuple(pl.BlockSpec(memory_space=pltpu.HBM if i in hbm else pltpu.VMEM) for i in range(len(outs))),
        scratch_shapes=list(scratch),
        input_output_aliases=alias or {},
        compiler_params=pltpu.CompilerParams(vmem_limit_bytes=int(room * 1.02) + extra),
        cost_estimate=pl.CostEstimate(flops=int(flops), bytes_accessed=int(nbytes), transcendentals=0),
    )(*arrays)


def sds(shape, dtype):
    return jax.ShapeDtypeStruct(shape, dtype)


def by_rows(count, chunk, fn):
    def step(i, carry):
        fn(pl.ds(pl.multiple_of(i * chunk, chunk), chunk))
        return carry

    lax.fori_loop(0, count // chunk, step, 0, unroll=True)


def lanes(i, width):
    return pl.ds(pl.multiple_of(i * width, width), width)


def partner(v):
    low = iota(v.shape, 1) % HEAD < ROT // 2
    return jnp.where(low, pltpu.roll(v, v.shape[1] - ROT // 2, 1), pltpu.roll(v, ROT // 2, 1))


def split_heads(v):
    first = iota(v.shape, 1) < HEAD
    zero = jnp.zeros_like(v)
    return jnp.concatenate([jnp.where(first, v, zero), jnp.where(first, zero, v)], axis=0)


def stats(x):
    centre = jnp.mean(x, axis=-1, keepdims=True)
    centered = x - centre
    spread = jnp.mean(centered * centered, axis=-1, keepdims=True)
    return centered, lax.rsqrt(spread + 1e-05)


def make(n):
    R = n // NB
    assert R * NB == n and R & (R - 1) == 0

    def across(v, mask):
        return lax.ppermute(v, "dp", [(d, d ^ (mask * R)) for d in range(n)])

    def swap(v, mask):
        return lax.ppermute(v, "dp", [(d, d ^ mask) for d in range(n)])

    def gather_r(own, tag):
        half = own.shape[0] // 2
        got = [(0, 0, own)]
        if R == 8 and tag == "one":
            from_x, from_y = swap(own, 2), swap(own, 4)
            got += [(2, 0, from_x), (4, 0, from_y)]
            got.append((6, 0, swap(from_y[:half], 2)))
            got.append((6, half, swap(from_x[half:], 4)))
        else:
            for m in range(2, R, 2):
                got.append((m, 0, swap(own, m)))
        return got + [(m + 1, at, swap(v, 1)) for m, at, v in got]

    def on_device(
        block_in, grad_out, w_qkv, b_qkv, w_o, b_o, w_in, b_in, w_out, b_out,
        ln1_gain, ln1_shift, ln2_gain, ln2_shift, seq_lens, seq_device, seq_offset,
    ):
        T = block_in.shape[0]
        NT = NB * T
        rows = w_qkv.shape[0]
        ff_dev = w_out.shape[0]
        FB = w_in.shape[1] // NB
        W1 = 3 * QB + FB
        J = R // 2
        MF = NB * rows + ff_dev
        MA = NB * rows
        MS = MA + 8
        idx = lax.axis_index("dp").astype(I32)
        b, r = idx // R, idx % R
        br = jnp.stack([b, r])

        slots1 = jnp.arange(T, dtype=I32)
        owners = [(b ^ k) * R + r for k in range(NB)]
        device = jnp.concatenate([jnp.full((T,), o, I32) for o in owners])
        slots = jnp.tile(slots1, NB)
        count = seq_lens.shape[0]
        inside = (
            (seq_device[None, :] == device[:, None])
            & (slots[:, None] >= seq_offset[None, :])
            & (slots[:, None] < (seq_offset + seq_lens)[None, :])
        )
        number = jnp.arange(count, dtype=I32)
        present = jnp.any(inside, axis=1)
        segment = jnp.where(present, jnp.sum(jnp.where(inside, number[None, :], 0), axis=1), count + slots)
        position = jnp.sum(jnp.where(inside, slots[:, None] - seq_offset[None, :], 0), axis=1)
        live = present.astype(F32)[:, None]
        seg = segment.reshape(NB, T)
        allowed = (seg[:, :, None] == seg[:, None, :]) & (slots1[None, None, :] <= slots1[None, :, None])
        mask = jnp.where(allowed, 0.0, NEG).astype(F32)
        lane = jnp.arange(2 * HEAD, dtype=I32) % HEAD
        half = ROT // 2
        freqs = 10000.0 ** (-(lane % half).astype(F32) / half)
        angle = position.astype(F32)[:, None] * jnp.where(lane < ROT, freqs, 0.0)[None, :]
        cosine = jnp.cos(angle)
        sines = jnp.sin(angle) * jnp.where(lane < half, -1.0, 1.0)[None, :]

        small = [b_in, b_qkv, b_o, b_out, ln1_gain, ln1_shift, ln2_gain, ln2_shift]
        widths = [v.shape[0] for v in small]
        offsets = [sum(widths[:i]) for i in range(len(small))]
        WS = 1024

        def pack_body(br, qkv_ref, in_ref, o_ref, out_ref, *rest):
            vectors, outs = rest[: len(small)], rest[len(small) :]
            for k in range(NB):
                to = br[0] ^ k
                for s in range(3):
                    outs[k][:, s * QB : (s + 1) * QB] = qkv_ref[:, lanes(s * NB + to, QB)]
                outs[k][:, 3 * QB :] = in_ref[:, lanes(to, FB)]
            outs[NB][:ff_dev] = out_ref[...]
            outs[NB][ff_dev:] = o_ref[...]
            parts = [v[...].astype(F32) for v in vectors]
            if WS > sum(widths):
                parts.append(jnp.zeros((1, WS - sum(widths)), F32))
            every = jnp.concatenate(parts, axis=1)
            for i in range(8):
                outs[NB + 1][:, i] = jnp.broadcast_to(every[:, i * 128 : (i + 1) * 128], (n, 128)).astype(BF)

        packed = call(
            pack_body,
            [("s", br), ("v", w_qkv), ("v", w_in), ("v", w_o), ("v", w_out)] + [("v", v.reshape(1, -1)) for v in small],
            [sds((rows, W1), BF)] * NB + [sds((ff_dev + rows, D), BF), sds((n, 8, 128), BF)], extra=56 << 20,
        )
        columns, own_two, small_out = packed[:NB], packed[NB], packed[NB + 1]

        def blocks_of(own, after):
            two = across(after, 2)
            return [own, across(after, 1), two, across(two, 1)]

        two = gather_r(own_two, "two")
        crossed = [across(columns[k], k) for k in range(1, NB)]
        after, _ = lax.optimization_barrier((block_in, crossed))
        mine = jnp.concatenate([columns[0]] + crossed).reshape(NB, rows, W1)
        one = gather_r(mine, "one")
        tokens = blocks_of(block_in, after)
        small_in = lax.all_to_all(small_out, "dp", 0, 0, tiled=True)
        after, _ = lax.optimization_barrier((grad_out, tokens[1]))
        grads_in = [grad_out] + [across(after, k) for k in range(1, NB)]

        def pick(width_mod, off, base, width):
            return (iota((width, width_mod.shape[1]), 0) + base == off + width_mod).astype(BF)

        def window(off, width):
            base = off // 128 * 128
            return base, -(-(off + width) // 128) * 128 - base

        def dec_body(br, got, bq, bi, g1, s1, g2, s2, bo):
            def expand(which, col):
                width, off = widths[which], offsets[which]
                base, span = window(off, width)
                total = col.shape[1]
                sel = pick(lax.rem(col, width), off, base, span)
                every = dot_nn(jnp.concatenate([got[:, i] for i in range(base // 128, (base + span) // 128)], axis=1), sel)
                return jnp.sum(jnp.where(iota((n, total), 0) == lax.div(col, width), every, 0.0), axis=0, keepdims=True)

            at = iota((1, 3 * QB), 1)
            bq[...] = expand(1, lax.div(at, QB) * D + br[0] * QB + lax.rem(at, QB))
            bi[...] = expand(0, iota((1, FB), 1) + br[0] * FB)
            whole = iota((1, D), 1)
            bo[...] = expand(2, whole) + expand(3, whole)
            for ref, which in ((g1, 4), (s1, 5), (g2, 6), (s2, 7)):
                ref[...] = expand(which, whole)

        row = sds((1, D), F32)
        bias_qkv, bias_in, gain_one, shift_one, gain_two, shift_two, bias_o = call(
            dec_body, [("s", br), ("v", small_in)], [sds((1, 3 * QB), F32), sds((1, FB), F32)] + [row] * 5
        )

        def load_one(br, parts, w1, sems, low, high):
            cols = pl.ds(low, high - low)
            copies = []
            for (m, start, _), ref in zip(one, parts):
                for k in range(ref.shape[0]):
                    to = w1.at[br[0] ^ (start + k), br[1] ^ m, :, cols]
                    copies.append(pltpu.make_async_copy(ref.at[k, :, cols], to, sems.at[int(low > 0), len(copies)]))
            return copies

        def load_two(br, parts, wout, wo, sems):
            copies = []
            for (m, start, _), ref in zip(two, parts):
                size = ref.shape[0]
                for to, first, last in ((wout, 0, ff_dev), (wo, ff_dev, ff_dev + rows)):
                    low, high = max(start, first), min(start + size, last)
                    if low < high:
                        copies.append(
                            pltpu.make_async_copy(
                                ref.at[pl.ds(low - start, high - low)],
                                to.at[br[1] ^ m, pl.ds(low - first, high - low)],
                                sems.at[len(copies)],
                            )
                        )
            return copies

        dma = pltpu.SemaphoreType.DMA
        PAIRS = QB // 128

        def fwd_body(br, h0, h1, h2, h3, cos, sin, mask_ref, bq, bi, g1, s1, g2, s2, *rest):
            one_refs, two_refs, rest = rest[: len(one)], rest[len(one) : len(one) + len(two)], rest[len(one) + len(two) :]
            act1, act2, q, k, v, probs, mixed, hidden, dgelu, xhat_ref, w1, wo, wout, own, later, away = rest[:16]
            stage, x_ref, semx, sem1, sem2, semp = rest[16:]
            cx = [pltpu.make_async_copy(h, x_ref.at[i], semx.at[i]) for i, h in enumerate((h0, h1, h2, h3))]
            c1, c1f = load_one(br, one_refs, w1, sem1, 0, 3 * QB), load_one(br, one_refs, w1, sem1, 3 * QB, W1)
            c2 = load_two(br, two_refs, wout, wo, sem2)
            for c in cx + c1 + c1f + c2:
                c.start()
            for i in range(NB):
                cx[i].wait()

                def norm(rws, i=i):
                    centered, rstd = stats(x_ref[i, rws].astype(F32))
                    xhat = centered * rstd
                    to = pl.ds(pl.multiple_of(i * T + rws.start, T), T)
                    xhat_ref[to] = xhat
                    act1[to] = (xhat * g1[...] + s1[...]).astype(BF)
                    act2[to] = (xhat * g2[...] + s2[...]).astype(BF)

                by_rows(T, T, norm)
            for c in c1:
                c.wait()
            for s, ref in enumerate((q, k, v)):
                wt = w1[:, :, :, s * QB : (s + 1) * QB].reshape(D, QB)

                def project(rws, s=s, ref=ref, wt=wt):
                    y = dot_nn(act1[rws], wt) + bq[:, s * QB : (s + 1) * QB]
                    for p in range(PAIRS):
                        z = y[:, p * 128 : (p + 1) * 128]
                        if s < 2:
                            z = z * cos[rws] + partner(z) * sin[rws]
                        ref[rws, p * 128 : (p + 1) * 128] = z.astype(BF)

                by_rows(NT, 256, project)

            def attend(i, carry):
                rws = pl.ds(pl.multiple_of(i * T, T), T)
                m2 = mask_ref[i]
                m2 = jnp.concatenate([m2, m2], axis=0)
                for p in range(PAIRS):
                    cols = slice(p * 128, (p + 1) * 128)
                    s = dot_nt(split_heads(q[rws, cols]), k[rws, cols]) * (1.0 / math.sqrt(HEAD)) + m2
                    e = jnp.exp(s - jnp.max(s, axis=-1, keepdims=True))
                    pr = e / jnp.sum(e, axis=-1, keepdims=True)
                    probs[i * PAIRS + p] = pr
                    pb = pr.astype(BF)
                    pb = jnp.concatenate([pb[:T], pb[T:]], axis=1)
                    mixed[rws, cols] = dot_nn(pb, split_heads(v[rws, cols])).astype(BF)
                return carry

            lax.fori_loop(0, NB, attend, 0, unroll=True)
            for c in c1f:
                c.wait()

            def feed(t, carry):
                cols = lanes(t, 256)
                wt = w1[:, :, :, pl.ds(pl.multiple_of(3 * QB + t * 256, 256), 256)].reshape(D, 256)

                def act(rws):
                    h = dot_nn(act2[rws], wt) + bi[:, cols]
                    cdf = 0.5 * (1.0 + lax.erf(h * (1.0 / math.sqrt(2.0))))
                    hidden[rws, cols] = (h * cdf).astype(BF)
                    dgelu[rws, cols] = cdf + h * (jnp.exp(-0.5 * h * h) * (1.0 / math.sqrt(2.0 * math.pi)))

                by_rows(NT, 256, act)
                return carry

            lax.fori_loop(0, FB // 256, feed, 0, unroll=True)
            for c in c2:
                c.wait()

            def project_out(t, carry):
                cols = lanes(t, 256)
                y = dot_nn(mixed[...], wo[:, :, cols].reshape(QB, 256))
                y = y + dot_nn(hidden[...], wout[:, :, cols].reshape(FB, 256))
                own[:, cols] = y[:T]
                later[:, cols] = y[2 * T : 3 * T]
                stage[:T, cols] = y[T : 2 * T].astype(BF)
                stage[T:, cols] = y[3 * T :].astype(BF)
                return carry

            lax.fori_loop(0, D // 256, project_out, 0, unroll=True)
            send = pltpu.make_async_copy(stage, away, semp)
            send.start()
            send.wait()

        tab = sds((NT, D), BF)
        third = sds((NT, QB), BF)
        block = sds((T, D), BF)
        act1, act2, q, k, v, probs, mixed, hidden, dgelu, xhat, full_one, full_o, full_out, own_part, later_part, away_part = call(
            fwd_body,
            [("s", br)] + [("h", x) for x in tokens]
            + [("v", a) for a in (cosine, sines, mask, bias_qkv, bias_in, gain_one, shift_one, gain_two, shift_two)]
            + [("h", a) for _, _, a in one + two],
            [tab, tab, third, third, third, sds((NB * PAIRS, 2 * T, T), F32), third, sds((NT, FB), BF), sds((NT, FB), F32),
             sds((NT, D), F32), sds((NB, R, rows, W1), BF), sds((R, rows, D), BF), sds((R, ff_dev, D), BF),
             sds((T, D), F32), sds((T, D), F32), sds((2 * T, D), BF)],
            [pltpu.VMEM((2 * T, D), BF), pltpu.VMEM((NB, T, D), BF), dma((NB,)), dma((2, R * NB)), dma((3 * R,)), dma],
            hbm=(15,),
            flops=2 * NT * D * W1 + 2 * NT * D * (QB + FB) + 8 * NT * T * QB,
        )

        got_one = across(away_part, 1)

        def pass_body(keep, got, out):
            def fn(rws):
                out[rws] = (keep[rws] + got[pl.ds(T, T)].astype(F32)).astype(BF)

            by_rows(T, T, fn)


        def bwd1_body(br, live_ref, g0, g1, g2, g3, act2, hidden, dgelu, wout, *rest):
            grad, dhid, keep, send, sum_in, term, flip = rest
            for i, g in enumerate((g0, g1, g2, g3)):

                def masked(rws, i=i, g=g):
                    to = pl.ds(pl.multiple_of(i * T + rws.start, T), T)
                    grad[to] = (g[rws].astype(F32) * live_ref[to]).astype(BF)

                by_rows(T, T, masked)

            def term_out(t, carry):
                flip[...] = hidden[:, lanes(t, 256)].T
                y = dot_nn(flip[...], grad[...])
                per = 256 // ff_dev
                term[pl.ds(t * per, per)] = y.reshape(per, ff_dev, D)
                return carry

            lax.fori_loop(0, FB // 256, term_out, 0, unroll=True)

            def to_out(j, carry):
                keep[j, MA:] = term[br[1] ^ (2 * j)]
                send[j, MA:] = term[br[1] ^ (2 * j + 1)].astype(BF)
                return carry

            lax.fori_loop(0, J, to_out, 0, unroll=True)

            def d_hidden(t, carry):
                cols = lanes(t, 256)
                per = 256 // ff_dev
                wt = wout[pl.ds(t * per, per)].reshape(256, D)
                y = (dot_nt(grad[...], wt) * dgelu[:, cols]).astype(BF)
                dhid[:, cols] = y
                sum_in[:, cols] = jnp.sum(y.astype(F32), axis=0, keepdims=True)
                return carry

            lax.fori_loop(0, FB // 256, d_hidden, 0, unroll=True)

            term_r = term.reshape(R * ff_dev // rows, rows, D) if ff_dev != rows else term

            def term_in(t, carry):
                flip[...] = act2[:, lanes(t, 256)].T
                term_r[:R] = dot_nn(flip[...], dhid[...]).reshape(R, rows, D)
                at = pl.ds(pl.multiple_of(t * rows, rows), rows)

                def one_j(j, carry):
                    keep[j, at] = term_r[br[1] ^ (2 * j)]
                    send[j, at] = term_r[br[1] ^ (2 * j + 1)].astype(BF)
                    return carry

                return lax.fori_loop(0, J, one_j, carry, unroll=True)

            lax.fori_loop(0, NB, term_in, 0, unroll=True)

        grad_r, dhid, keep_f, send_f, sum_in = call(
            bwd1_body,
            [("s", br), ("v", live)] + [("v", g) for g in grads_in] + [("v", a) for a in (act2, hidden, dgelu, full_out)],
            [tab, sds((NT, FB), BF), sds((J, MF, D), F32), sds((J, MF, D), BF), sds((1, FB), F32)],
            [pltpu.VMEM((R, ff_dev, D), F32), pltpu.VMEM((256, NT), BF)],
            flops=6 * NT * D * FB,
        )

        def bwd2_body(br, grad, mixed, act1, q, k, v, probs, cos, sin, wo, *rest):
            dqkv, keep, send, sum_qkv, dmix, term, term_o, flip = rest
            flip[...] = mixed[...].T
            term_o[...] = dot_nn(flip[...], grad[...]).reshape(R, rows, D)

            def to_o(j, carry):
                for c in range(NB):
                    cols = slice(c * QB, (c + 1) * QB)
                    keep[j, c * rows : (c + 1) * rows, 3 * QB :] = term_o[br[1] ^ (2 * j), :, cols]
                    send[j, c * rows : (c + 1) * rows, 3 * QB :] = term_o[br[1] ^ (2 * j + 1), :, cols].astype(BF)
                return carry

            lax.fori_loop(0, J, to_o, 0, unroll=True)
            dmix[...] = dot_nt(grad[...], wo[...].reshape(QB, D)).astype(BF)

            def attend(i, carry):
                rws = pl.ds(pl.multiple_of(i * T, T), T)
                for p in range(PAIRS):
                    cols = slice(p * 128, (p + 1) * 128)
                    pr = probs[i * PAIRS + p]
                    pb = pr.astype(BF)
                    dm2 = split_heads(dmix[rws, cols])
                    dp = dot_nt(dm2, v[rws, cols])
                    ds = (pr * (dp - jnp.sum(dp * pr, axis=-1, keepdims=True))).astype(BF)
                    dq = dot_nn(jnp.concatenate([ds[:T], ds[T:]], axis=1), split_heads(k[rws, cols]))
                    dk = dot_nn(ds.T, split_heads(q[rws, cols]))
                    dv = dot_nn(pb.T, dm2)
                    for s, z in enumerate((dq, dk)):
                        z = z * (1.0 / math.sqrt(HEAD))
                        z = z * cos[rws] - partner(z) * sin[rws]
                        dqkv[rws, s * QB + p * 128 : s * QB + (p + 1) * 128] = z.astype(BF)
                    dqkv[rws, 2 * QB + p * 128 : 2 * QB + (p + 1) * 128] = dv.astype(BF)
                return carry

            lax.fori_loop(0, NB, attend, 0, unroll=True)
            sum_qkv[...] = jnp.sum(dqkv[...].astype(F32), axis=0, keepdims=True)

            def term_qkv(t, carry):
                flip[...] = act1[:, lanes(t, 256)].T
                term[...] = dot_nn(flip[...], dqkv[...]).reshape(R, rows, 3 * QB)
                at = pl.ds(pl.multiple_of(t * rows, rows), rows)

                def one_j(j, carry):
                    keep[j, at, : 3 * QB] = term[br[1] ^ (2 * j)]
                    send[j, at, : 3 * QB] = term[br[1] ^ (2 * j + 1)].astype(BF)
                    return carry

                return lax.fori_loop(0, J, one_j, carry, unroll=True)

            lax.fori_loop(0, NB, term_qkv, 0, unroll=True)

        dqkv, keep_a, send_a, sum_qkv = call(
            bwd2_body,
            [("s", br)] + [("v", a) for a in (grad_r, mixed, act1, q, k, v, probs, cosine, sines, full_o)],
            [sds((NT, 3 * QB), BF), sds((J, MS, D), F32), sds((J, MS, D), BF), sds((1, 3 * QB), F32)],
            [pltpu.VMEM((NT, QB), BF), pltpu.VMEM((R, rows, 3 * QB), F32), pltpu.VMEM((R, rows, D), F32),
             pltpu.VMEM((256, NT), BF)],
            flops=2 * NT * D * (3 * QB + 2 * QB) + 16 * NT * T * QB,
        )

        def merge_body(extra, keep, got, *rest):
            size = keep.shape[1]
            outs = rest[extra:]
            if extra:
                pass_body(*rest[:extra], outs[J])
            for j in range(J):

                def fn(rws, j=j):
                    y = keep[j, rws] + got[j, rws].astype(F32)
                    outs[j][rws] = y if j == 0 else y.astype(BF)

                by_rows(size, size, fn)

        def merge(keep, send, passed=()):
            size = keep.shape[1]
            got = swap(send, 1)
            outs = call(
                functools.partial(merge_body, len(passed)), [("v", a) for a in (keep, got, *passed)],
                [sds((size, D), F32)] + [sds((size, D), BF)] * (J - 1) + [block] * bool(passed),
            )
            return [outs[0]] + [swap(outs[j], 2 * j) for j in range(1, J)], outs[J:]

        merged_f, (pass_part,) = merge(keep_f, send_f, (later_part, got_one))
        got_two = across(pass_part, 2)
        out_widths = [FB * NB // n, 3 * D // n] + [D // n] * 5
        out_offsets = [sum(out_widths[:i]) for i in range(len(out_widths))]
        WO = -(-sum(out_widths) // 128) * 128

        def bwd3_body(br, xhat, w1, dqkv, dhid, grad, sum_in, sum_qkv, g1, g2, keep_in, send_in, *rest):
            own, later, away, keep, send, stage, gs, sums, tot, semp = rest
            gs[...] = jnp.sum(grad[:T].astype(F32), axis=0, keepdims=True)

            def back(t, carry):
                cols = lanes(t, QB)
                d1 = dot_nt(dqkv[...], w1[t, :, :, : 3 * QB].reshape(QB, 3 * QB))
                d2 = dot_nt(dhid[...], w1[t, :, :, 3 * QB :].reshape(QB, FB))
                xh = xhat[:, cols]
                y = d1 * g1[:, cols] + d2 * g2[:, cols]
                own[:, cols] = y[:T]
                later[:, cols] = y[2 * T : 3 * T]
                stage[:T, cols] = y[T : 2 * T].astype(BF)
                stage[T:, cols] = y[3 * T :].astype(BF)
                for i, z in enumerate((d1 * xh, d1, d2 * xh, d2)):
                    sums[i : i + 1, cols] = jnp.sum(z, axis=0, keepdims=True)
                return carry

            lax.fori_loop(0, D // QB, back, 0, unroll=True)
            sending = pltpu.make_async_copy(stage, away, semp)
            sending.start()

            total = jnp.zeros((n, WO), F32)

            def place(total, vec, col, which):
                size = vec.shape[1]
                width, off = out_widths[which], out_offsets[which]
                mine = jnp.where(iota((n, size), 0) == lax.div(col, width), vec, 0.0)
                base = off // 128 * 128
                span = -(-(off + width) // 128) * 128 - base
                sel = pick(lax.rem(col, width), off, base, span)
                high = mine.astype(BF)
                low = (mine - high.astype(F32)).astype(BF)
                placed = dot_nt(high, sel) + dot_nt(low, sel)
                parts = []
                if base:
                    parts.append(jnp.zeros((n, base), F32))
                parts.append(placed)
                if base + span < WO:
                    parts.append(jnp.zeros((n, WO - base - span), F32))
                return total + (jnp.concatenate(parts, axis=1) if len(parts) > 1 else placed)

            whole = iota((1, D), 1)
            at = iota((1, 3 * QB), 1)
            total = place(total, sum_in[...], iota((1, FB), 1) + br[0] * FB, 0)
            total = place(total, sum_qkv[...], lax.div(at, QB) * D + br[0] * QB + lax.rem(at, QB), 1)
            total = place(total, gs[...], whole, 2)
            for i in range(4):
                total = place(total, sums[i : i + 1], whole, 3 + i)
            tot[...] = total
            for j in range(J):
                for ref, m in ((keep, 2 * j), (send, 2 * j + 1)):
                    lines = [tot[pl.ds(to * R + (br[1] ^ m), 1), :] for to in range(NB)]
                    lines.append(jnp.zeros((MS - MA - NB, WO), F32))
                    ref[j, MA:, :WO] = jnp.concatenate(lines, axis=0).astype(ref.dtype)
            sending.wait()

        own_g, later_g, away_g, keep_a, send_a = call(
            bwd3_body,
            [("s", br)] + [("v", a) for a in (xhat, full_one, dqkv, dhid, grad_r, sum_in, sum_qkv, gain_one, gain_two, keep_a, send_a)],
            [sds((T, D), F32), sds((T, D), F32), sds((2 * T, D), BF), sds((J, MS, D), F32), sds((J, MS, D), BF)],
            [pltpu.VMEM((2 * T, D), BF), pltpu.VMEM((1, D), F32), pltpu.VMEM((8, D), F32), pltpu.VMEM((n, WO), F32), dma], hbm=(2,),
            alias={10: 3, 11: 4},
            flops=2 * NT * D * W1,
        )
        back_one = across(away_g, 1)
        (pass_g,) = call(pass_body, [("v", later_g), ("v", back_one)], [block])
        back_two = across(pass_g, 2)
        merged_a, _ = merge(keep_a, send_a)

        def total_body(x, live_ref, bo, own, p1, p2, out):
            def fn(rws):
                y = x[rws].astype(F32) + bo[...] + own[rws] + p1[rws].astype(F32) + p2[rws].astype(F32)
                out[rws] = (y * live_ref[rws]).astype(BF)

            by_rows(T, T, fn)

        def plane_f_body(br, x, live_ref, bo, own, p1, p2, *rest):
            got, (w_out_ref, z0, z1, z2, z3, out) = rest[:J], rest[J:]
            total_body(x, live_ref, bo, own, p1, p2, out)

            def out_rows(rws):
                y = got[0][pl.ds(pl.multiple_of(MA + rws.start, 8), rws.size)]
                for ref in got[1:]:
                    y = y + ref[pl.ds(pl.multiple_of(MA + rws.start, 8), rws.size)].astype(F32)
                w_out_ref[rws] = y

            by_rows(ff_dev, min(32, ff_dev), out_rows)
            for k, ref in enumerate((z0, z1, z2, z3)):
                at = pl.ds(pl.multiple_of((br[0] ^ k) * rows, rows), rows)
                y = got[0][at]
                for other in got[1:]:
                    y = y + other[at].astype(F32)
                ref[...] = y if k == 0 else y.astype(BF)

        grad_w_out, zf0, *zf, block_out = call(
            plane_f_body,
            [("s", br)] + [("v", a) for a in (block_in, live[:T], bias_o, own_part, got_one, got_two, *merged_f)],
            [sds((ff_dev, D), F32), sds((rows, FB), F32)] + [sds((rows, FB), BF)] * 3 + [block],
        )

        def plane_a_body(br, *rest):
            got, (w_o_ref, z0, z1, z2, z3) = rest[:J], rest[J:]
            for c in range(NB):
                y = got[0][c * rows : (c + 1) * rows, 3 * QB :]
                for other in got[1:]:
                    y = y + other[c * rows : (c + 1) * rows, 3 * QB :].astype(F32)
                w_o_ref[:, c * QB : (c + 1) * QB] = y
            for k, ref in enumerate((z0, z1, z2, z3)):
                at = pl.ds(pl.multiple_of((br[0] ^ k) * rows, rows), rows)
                y = got[0][at, : 3 * QB]
                for other in got[1:]:
                    y = y + other[at, : 3 * QB].astype(F32)
                ref[:rows] = y if k == 0 else y.astype(BF)
                y = got[0][MA:, :WO]
                for other in got[1:]:
                    y = y + other[MA:, :WO].astype(F32)
                y = jnp.sum(jnp.where(iota(y.shape, 0) == (br[0] ^ k), y, 0.0), axis=0, keepdims=True)
                ref[rows:, :WO] = jnp.broadcast_to(y, (8, WO)).astype(ref.dtype)

        grad_w_o, za0, *za = call(
            plane_a_body, [("s", br)] + [("v", a) for a in merged_a],
            [sds((rows, D), F32), sds((rows + 8, 3 * QB), F32)] + [sds((rows + 8, 3 * QB), BF)] * 3,
        )
        zf = [zf0] + [across(z, k + 1) for k, z in enumerate(zf)]
        za = [za0] + [across(z, k + 1) for k, z in enumerate(za)]

        def place_f_body(br, z0, z1, z2, z3, out):
            for k, ref in enumerate((z0, z1, z2, z3)):
                out[:, lanes(br[0] ^ k, FB)] = ref[...].astype(F32)

        small_order = (0, 1, 2, 2, 3, 4, 5, 6)

        def place_a_body(br, z0, z1, z2, z3, out, *small):
            y = sum(ref[rows:, :WO].astype(F32) for ref in (z0, z1, z2, z3))
            for ref, which in zip(small, small_order):
                ref[...] = y[:1, out_offsets[which] : out_offsets[which] + out_widths[which]]
            for k, ref in enumerate((z0, z1, z2, z3)):
                at = br[0] ^ k
                for s in range(3):
                    out[:, lanes(s * NB + at, QB)] = ref[:rows, s * QB : (s + 1) * QB].astype(F32)

        def input_body(x, grad, own, p1, p2, out):
            def fn(rws):
                centered, rstd = stats(x[rws].astype(F32))
                xh = centered * rstd
                g = own[rws] + p1[rws].astype(F32) + p2[rws].astype(F32)
                mean_g = jnp.mean(g, axis=-1, keepdims=True)
                mean_gx = jnp.mean(g * xh, axis=-1, keepdims=True)
                out[rws] = (grad[rws].astype(F32) + rstd * (g - mean_g - xh * mean_gx)).astype(BF)

            by_rows(T, T, fn)

        def final_body(br, *rest):
            ins, outs = rest[:13], rest[13:]
            place_f_body(br, *ins[5:9], outs[1])
            input_body(*ins[:5], outs[0])
            place_a_body(br, *ins[9:13], *outs[2:])

        grad_input, grad_w_in, grad_w_qkv, *outs = call(
            final_body,
            [("s", br)] + [("v", a) for a in (block_in, grad_r[:T], own_g, back_one, back_two, *zf, *za)],
            [block, sds((rows, NB * FB), F32), sds((rows, 3 * D), F32)] + [sds((1, out_widths[i]), F32) for i in small_order],
        )
        outs = [o.reshape(-1) for o in outs]

        grad_b_in, grad_b_qkv, grad_b_o, grad_b_out, grad_g1, grad_s1, grad_g2, grad_s2 = outs
        return (
            block_out, grad_input, grad_w_qkv, grad_b_qkv, grad_w_o, grad_b_o, grad_w_in, grad_b_in,
            grad_w_out, grad_b_out, grad_g1, grad_s1, grad_g2, grad_s2,
        )

    return on_device


def solution(mesh):
    two, one = P("dp", None), P("dp")
    n = mesh.shape["dp"]
    on_device = make(n)

    return jax.shard_map(
        on_device,
        mesh=mesh,
        in_specs=(two, two, two, one, two, one, two, one, two, one, one, one, one, one, P(), P(), P()),
        out_specs=(two, two, two, one, two, one, two, one, two, one, one, one, one, one),
        check_vma=False,
    )
```

```python
import math

import jax
import jax.numpy as jnp
from jax import lax
from jax.experimental import pallas as pl
from jax.experimental.pallas import tpu as pltpu
from jax.sharding import PartitionSpec as P


D = 1024
HEAD = 64
ROT = 16
NB = 4
QB = D // NB
NEG = -1e30
SHARE = 1.0

F32 = jnp.float32
BF = jnp.bfloat16
I32 = jnp.int32


def dot_nn(left, right):
    return jnp.dot(left, right, preferred_element_type=F32)


def dot_nt(left, right):
    return lax.dot_general(left, right, (((1,), (1,)), ((), ())), preferred_element_type=F32)


def iota(shape, axis):
    return lax.broadcasted_iota(I32, shape, axis)


def call(body, ins, outs, scratch=(), flops=0, extra=4 << 20, hbm=(), alias=None):
    spaces = {"v": pltpu.VMEM, "s": pltpu.SMEM, "a": pl.ANY, "h": pltpu.HBM}
    arrays = [a for _, a in ins]
    nbytes = sum(a.size * a.dtype.itemsize for a in arrays) + sum(math.prod(o.shape) * o.dtype.itemsize for o in outs)
    room = sum(math.prod(t.shape) * jnp.dtype(t.dtype).itemsize for t in scratch if getattr(t, "memory_space", None) == pltpu.VMEM)
    room += SHARE * (sum(a.size * a.dtype.itemsize for s, a in ins if s == "v") + sum(math.prod(o.shape) * o.dtype.itemsize for i, o in enumerate(outs) if i not in hbm))
    return pl.pallas_call(
        body,
        out_shape=tuple(outs),
        in_specs=[pl.BlockSpec(memory_space=spaces[s]) for s, _ in ins],
        out_specs=tuple(pl.BlockSpec(memory_space=pltpu.HBM if i in hbm else pltpu.VMEM) for i in range(len(outs))),
        scratch_shapes=list(scratch),
        input_output_aliases=alias or {},
        compiler_params=pltpu.CompilerParams(vmem_limit_bytes=int(room * 1.02) + extra),
        cost_estimate=pl.CostEstimate(flops=int(flops), bytes_accessed=int(nbytes), transcendentals=0),
    )(*arrays)


def sds(shape, dtype):
    return jax.ShapeDtypeStruct(shape, dtype)


def by_rows(count, chunk, fn):
    def step(i, carry):
        fn(pl.ds(pl.multiple_of(i * chunk, chunk), chunk))
        return carry

    lax.fori_loop(0, count // chunk, step, 0, unroll=True)


def lanes(i, width):
    return pl.ds(pl.multiple_of(i * width, width), width)


def partner(v):
    low = iota(v.shape, 1) % HEAD < ROT // 2
    return jnp.where(low, pltpu.roll(v, v.shape[1] - ROT // 2, 1), pltpu.roll(v, ROT // 2, 1))


def split_heads(v):
    first = iota(v.shape, 1) < HEAD
    zero = jnp.zeros_like(v)
    return jnp.concatenate([jnp.where(first, v, zero), jnp.where(first, zero, v)], axis=0)


def stats(x):
    centre = jnp.mean(x, axis=-1, keepdims=True)
    centered = x - centre
    spread = jnp.mean(centered * centered, axis=-1, keepdims=True)
    return centered, lax.rsqrt(spread + 1e-05)


def make(n):
    R = n // NB
    assert R * NB == n and R & (R - 1) == 0

    def across(v, mask):
        return lax.ppermute(v, "dp", [(d, d ^ (mask * R)) for d in range(n)])

    def swap(v, mask):
        return lax.ppermute(v, "dp", [(d, d ^ mask) for d in range(n)])

    def gather_r(own, tag):
        half = own.shape[0] // 2
        got = [(0, 0, own)]
        if R == 8 and tag == "one":
            from_x, from_y = swap(own, 2), swap(own, 4)
            got += [(2, 0, from_x), (4, 0, from_y)]
            got.append((6, 0, swap(from_y[:half], 2)))
            got.append((6, half, swap(from_x[half:], 4)))
        else:
            for m in range(2, R, 2):
                got.append((m, 0, swap(own, m)))
        return got + [(m + 1, at, swap(v, 1)) for m, at, v in got]

    def on_device(
        block_in, grad_out, w_qkv, b_qkv, w_o, b_o, w_in, b_in, w_out, b_out,
        ln1_gain, ln1_shift, ln2_gain, ln2_shift, seq_lens, seq_device, seq_offset,
    ):
        T = block_in.shape[0]
        NT = NB * T
        rows = w_qkv.shape[0]
        ff_dev = w_out.shape[0]
        FB = w_in.shape[1] // NB
        W1 = 3 * QB + FB
        J = R // 2
        MF = NB * rows + ff_dev
        MA = NB * rows
        MS = MA + 8
        idx = lax.axis_index("dp").astype(I32)
        b, r = idx // R, idx % R
        br = jnp.stack([b, r])

        slots1 = jnp.arange(T, dtype=I32)
        owners = [(b ^ k) * R + r for k in range(NB)]
        device = jnp.concatenate([jnp.full((T,), o, I32) for o in owners])
        slots = jnp.tile(slots1, NB)
        count = seq_lens.shape[0]
        inside = (
            (seq_device[None, :] == device[:, None])
            & (slots[:, None] >= seq_offset[None, :])
            & (slots[:, None] < (seq_offset + seq_lens)[None, :])
        )
        number = jnp.arange(count, dtype=I32)
        present = jnp.any(inside, axis=1)
        segment = jnp.where(present, jnp.sum(jnp.where(inside, number[None, :], 0), axis=1), count + slots)
        position = jnp.sum(jnp.where(inside, slots[:, None] - seq_offset[None, :], 0), axis=1)
        live = present.astype(F32)[:, None]
        seg = segment.reshape(NB, T)
        allowed = (seg[:, :, None] == seg[:, None, :]) & (slots1[None, None, :] <= slots1[None, :, None])
        mask = jnp.where(allowed, 0.0, NEG).astype(F32)
        lane = jnp.arange(2 * HEAD, dtype=I32) % HEAD
        half = ROT // 2
        freqs = 10000.0 ** (-(lane % half).astype(F32) / half)
        angle = position.astype(F32)[:, None] * jnp.where(lane < ROT, freqs, 0.0)[None, :]
        cosine = jnp.cos(angle)
        sines = jnp.sin(angle) * jnp.where(lane < half, -1.0, 1.0)[None, :]

        small = [b_in, b_qkv, b_o, b_out, ln1_gain, ln1_shift, ln2_gain, ln2_shift]
        widths = [v.shape[0] for v in small]
        offsets = [sum(widths[:i]) for i in range(len(small))]
        WS = 1024

        def pack_body(br, qkv_ref, in_ref, o_ref, out_ref, *rest):
            vectors, outs = rest[: len(small)], rest[len(small) :]
            for k in range(NB):
                to = br[0] ^ k
                for s in range(3):
                    outs[k][:, s * QB : (s + 1) * QB] = qkv_ref[:, lanes(s * NB + to, QB)]
                outs[k][:, 3 * QB :] = in_ref[:, lanes(to, FB)]
            outs[NB][:ff_dev] = out_ref[...]
            outs[NB][ff_dev:] = o_ref[...]
            parts = [v[...].astype(F32) for v in vectors]
            if WS > sum(widths):
                parts.append(jnp.zeros((1, WS - sum(widths)), F32))
            every = jnp.concatenate(parts, axis=1)
            for i in range(8):
                outs[NB + 1][:, i] = jnp.broadcast_to(every[:, i * 128 : (i + 1) * 128], (n, 128)).astype(BF)

        packed = call(
            pack_body,
            [("s", br), ("v", w_qkv), ("v", w_in), ("v", w_o), ("v", w_out)] + [("v", v.reshape(1, -1)) for v in small],
            [sds((rows, W1), BF)] * NB + [sds((ff_dev + rows, D), BF), sds((n, 8, 128), BF)], extra=56 << 20,
        )
        columns, own_two, small_out = packed[:NB], packed[NB], packed[NB + 1]

        def blocks_of(own, after):
            two = across(after, 2)
            return [own, across(after, 1), two, across(two, 1)]

        two = gather_r(own_two, "two")
        crossed = [across(columns[k], k) for k in range(1, NB)]
        after, _ = lax.optimization_barrier((block_in, crossed))
        mine = jnp.concatenate([columns[0]] + crossed).reshape(NB, rows, W1)
        one = gather_r(mine, "one")
        tokens = blocks_of(block_in, after)
        small_in = lax.all_to_all(small_out, "dp", 0, 0, tiled=True)
        after, _ = lax.optimization_barrier((grad_out, tokens[1]))
        grads_in = blocks_of(grad_out, after)

        def pick(width_mod, off, base, width):
            return (iota((width, width_mod.shape[1]), 0) + base == off + width_mod).astype(BF)

        def window(off, width):
            base = off // 128 * 128
            return base, -(-(off + width) // 128) * 128 - base

        def dec_body(br, got, bq, bi, g1, s1, g2, s2, bo):
            def expand(which, col):
                width, off = widths[which], offsets[which]
                base, span = window(off, width)
                total = col.shape[1]
                sel = pick(lax.rem(col, width), off, base, span)
                every = dot_nn(jnp.concatenate([got[:, i] for i in range(base // 128, (base + span) // 128)], axis=1), sel)
                return jnp.sum(jnp.where(iota((n, total), 0) == lax.div(col, width), every, 0.0), axis=0, keepdims=True)

            at = iota((1, 3 * QB), 1)
            bq[...] = expand(1, lax.div(at, QB) * D + br[0] * QB + lax.rem(at, QB))
            bi[...] = expand(0, iota((1, FB), 1) + br[0] * FB)
            whole = iota((1, D), 1)
            bo[...] = expand(2, whole) + expand(3, whole)
            for ref, which in ((g1, 4), (s1, 5), (g2, 6), (s2, 7)):
                ref[...] = expand(which, whole)

        row = sds((1, D), F32)
        bias_qkv, bias_in, gain_one, shift_one, gain_two, shift_two, bias_o = call(
            dec_body, [("s", br), ("v", small_in)], [sds((1, 3 * QB), F32), sds((1, FB), F32)] + [row] * 5
        )

        def load_one(br, parts, w1, sems, low, high):
            cols = pl.ds(low, high - low)
            copies = []
            for (m, start, _), ref in zip(one, parts):
                for k in range(ref.shape[0]):
                    to = w1.at[br[0] ^ (start + k), br[1] ^ m, :, cols]
                    copies.append(pltpu.make_async_copy(ref.at[k, :, cols], to, sems.at[int(low > 0), len(copies)]))
            return copies

        def load_two(br, parts, wout, wo, sems):
            copies = []
            for (m, start, _), ref in zip(two, parts):
                size = ref.shape[0]
                for to, first, last in ((wout, 0, ff_dev), (wo, ff_dev, ff_dev + rows)):
                    low, high = max(start, first), min(start + size, last)
                    if low < high:
                        copies.append(
                            pltpu.make_async_copy(
                                ref.at[pl.ds(low - start, high - low)],
                                to.at[br[1] ^ m, pl.ds(low - first, high - low)],
                                sems.at[len(copies)],
                            )
                        )
            return copies

        dma = pltpu.SemaphoreType.DMA
        PAIRS = QB // 128

        def fwd_body(br, h0, h1, h2, h3, cos, sin, mask_ref, bq, bi, g1, s1, g2, s2, *rest):
            one_refs, two_refs, rest = rest[: len(one)], rest[len(one) : len(one) + len(two)], rest[len(one) + len(two) :]
            act1, act2, q, k, v, probs, mixed, hidden, dgelu, xhat_ref, w1, wo, wout, own, later, away = rest[:16]
            stage, x_ref, semx, sem1, sem2, semp = rest[16:]
            cx = [pltpu.make_async_copy(h, x_ref.at[i], semx.at[i]) for i, h in enumerate((h0, h1, h2, h3))]
            c1, c1f = load_one(br, one_refs, w1, sem1, 0, 3 * QB), load_one(br, one_refs, w1, sem1, 3 * QB, W1)
            c2 = load_two(br, two_refs, wout, wo, sem2)
            for c in cx + c1 + c1f + c2:
                c.start()
            for i in range(NB):
                cx[i].wait()

                def norm(rws, i=i):
                    centered, rstd = stats(x_ref[i, rws].astype(F32))
                    xhat = centered * rstd
                    to = pl.ds(pl.multiple_of(i * T + rws.start, T), T)
                    xhat_ref[to] = xhat
                    act1[to] = (xhat * g1[...] + s1[...]).astype(BF)
                    act2[to] = (xhat * g2[...] + s2[...]).astype(BF)

                by_rows(T, T, norm)
            for c in c1:
                c.wait()
            for s, ref in enumerate((q, k, v)):
                wt = w1[:, :, :, s * QB : (s + 1) * QB].reshape(D, QB)

                def project(rws, s=s, ref=ref, wt=wt):
                    y = dot_nn(act1[rws], wt) + bq[:, s * QB : (s + 1) * QB]
                    for p in range(PAIRS):
                        z = y[:, p * 128 : (p + 1) * 128]
                        if s < 2:
                            z = z * cos[rws] + partner(z) * sin[rws]
                        ref[rws, p * 128 : (p + 1) * 128] = z.astype(BF)

                by_rows(NT, 256, project)

            def attend(i, carry):
                rws = pl.ds(pl.multiple_of(i * T, T), T)
                m2 = mask_ref[i]
                m2 = jnp.concatenate([m2, m2], axis=0)
                for p in range(PAIRS):
                    cols = slice(p * 128, (p + 1) * 128)
                    s = dot_nt(split_heads(q[rws, cols]), k[rws, cols]) * (1.0 / math.sqrt(HEAD)) + m2
                    e = jnp.exp(s - jnp.max(s, axis=-1, keepdims=True))
                    pr = e / jnp.sum(e, axis=-1, keepdims=True)
                    probs[i * PAIRS + p] = pr
                    pb = pr.astype(BF)
                    pb = jnp.concatenate([pb[:T], pb[T:]], axis=1)
                    mixed[rws, cols] = dot_nn(pb, split_heads(v[rws, cols])).astype(BF)
                return carry

            lax.fori_loop(0, NB, attend, 0, unroll=True)
            for c in c1f:
                c.wait()

            def feed(t, carry):
                cols = lanes(t, 256)
                wt = w1[:, :, :, pl.ds(pl.multiple_of(3 * QB + t * 256, 256), 256)].reshape(D, 256)

                def act(rws):
                    h = dot_nn(act2[rws], wt) + bi[:, cols]
                    cdf = 0.5 * (1.0 + lax.erf(h * (1.0 / math.sqrt(2.0))))
                    hidden[rws, cols] = (h * cdf).astype(BF)
                    dgelu[rws, cols] = cdf + h * (jnp.exp(-0.5 * h * h) * (1.0 / math.sqrt(2.0 * math.pi)))

                by_rows(NT, 256, act)
                return carry

            lax.fori_loop(0, FB // 256, feed, 0, unroll=True)
            for c in c2:
                c.wait()

            def project_out(t, carry):
                cols = lanes(t, 256)
                y = dot_nn(mixed[...], wo[:, :, cols].reshape(QB, 256))
                y = y + dot_nn(hidden[...], wout[:, :, cols].reshape(FB, 256))
                own[:, cols] = y[:T]
                later[:, cols] = y[2 * T : 3 * T]
                stage[:T, cols] = y[T : 2 * T].astype(BF)
                stage[T:, cols] = y[3 * T :].astype(BF)
                return carry

            lax.fori_loop(0, D // 256, project_out, 0, unroll=True)
            send = pltpu.make_async_copy(stage, away, semp)
            send.start()
            send.wait()

        tab = sds((NT, D), BF)
        third = sds((NT, QB), BF)
        block = sds((T, D), BF)
        act1, act2, q, k, v, probs, mixed, hidden, dgelu, xhat, full_one, full_o, full_out, own_part, later_part, away_part = call(
            fwd_body,
            [("s", br)] + [("h", x) for x in tokens]
            + [("v", a) for a in (cosine, sines, mask, bias_qkv, bias_in, gain_one, shift_one, gain_two, shift_two)]
            + [("h", a) for _, _, a in one + two],
            [tab, tab, third, third, third, sds((NB * PAIRS, 2 * T, T), F32), third, sds((NT, FB), BF), sds((NT, FB), F32),
             sds((NT, D), F32), sds((NB, R, rows, W1), BF), sds((R, rows, D), BF), sds((R, ff_dev, D), BF),
             sds((T, D), F32), sds((T, D), F32), sds((2 * T, D), BF)],
            [pltpu.VMEM((2 * T, D), BF), pltpu.VMEM((NB, T, D), BF), dma((NB,)), dma((2, R * NB)), dma((3 * R,)), dma],
            hbm=(15,),
            flops=2 * NT * D * W1 + 2 * NT * D * (QB + FB) + 8 * NT * T * QB,
        )

        got_one = across(away_part, 1)

        def pass_body(keep, got, out):
            def fn(rws):
                out[rws] = (keep[rws] + got[pl.ds(T, T)].astype(F32)).astype(BF)

            by_rows(T, T, fn)


        def bwd2_body(br, live_ref, g0, g1, g2, g3, hidden, mixed, act1, q, k, v, probs, cos, sin, wo, *rest):
            grad, dqkv, keep, send, sum_qkv, dmix, term, term_o, term_out_ref, flip = rest
            for i, g in enumerate((g0, g1, g2, g3)):

                def masked(rws, i=i, g=g):
                    to = pl.ds(pl.multiple_of(i * T + rws.start, T), T)
                    grad[to] = (g[rws].astype(F32) * live_ref[to]).astype(BF)

                by_rows(T, T, masked)

            def term_out(t, carry):
                flip[...] = hidden[:, lanes(t, 256)].T
                y = dot_nn(flip[...], grad[...])
                per = 256 // ff_dev
                term_out_ref[pl.ds(t * per, per)] = y.reshape(per, ff_dev, D)
                return carry

            lax.fori_loop(0, FB // 256, term_out, 0, unroll=True)

            def to_out(j, carry):
                keep[j, MA:] = term_out_ref[br[1] ^ (2 * j)]
                send[j, MA:] = term_out_ref[br[1] ^ (2 * j + 1)].astype(BF)
                return carry

            lax.fori_loop(0, J, to_out, 0, unroll=True)

            flip[...] = mixed[...].T
            term_o[...] = dot_nn(flip[...], grad[...]).reshape(R, rows, D)

            def to_o(j, carry):
                for c in range(NB):
                    cols = slice(c * QB, (c + 1) * QB)
                    keep[j, c * rows : (c + 1) * rows, 3 * QB :] = term_o[br[1] ^ (2 * j), :, cols]
                    send[j, c * rows : (c + 1) * rows, 3 * QB :] = term_o[br[1] ^ (2 * j + 1), :, cols].astype(BF)
                return carry

            lax.fori_loop(0, J, to_o, 0, unroll=True)
            dmix[...] = dot_nt(grad[...], wo[...].reshape(QB, D)).astype(BF)

            def attend(i, carry):
                rws = pl.ds(pl.multiple_of(i * T, T), T)
                for p in range(PAIRS):
                    cols = slice(p * 128, (p + 1) * 128)
                    pr = probs[i * PAIRS + p]
                    pb = pr.astype(BF)
                    dm2 = split_heads(dmix[rws, cols])
                    dp = dot_nt(dm2, v[rws, cols])
                    ds = (pr * (dp - jnp.sum(dp * pr, axis=-1, keepdims=True))).astype(BF)
                    dq = dot_nn(jnp.concatenate([ds[:T], ds[T:]], axis=1), split_heads(k[rws, cols]))
                    dk = dot_nn(ds.T, split_heads(q[rws, cols]))
                    dv = dot_nn(pb.T, dm2)
                    for s, z in enumerate((dq, dk)):
                        z = z * (1.0 / math.sqrt(HEAD))
                        z = z * cos[rws] - partner(z) * sin[rws]
                        dqkv[rws, s * QB + p * 128 : s * QB + (p + 1) * 128] = z.astype(BF)
                    dqkv[rws, 2 * QB + p * 128 : 2 * QB + (p + 1) * 128] = dv.astype(BF)
                return carry

            lax.fori_loop(0, NB, attend, 0, unroll=True)
            sum_qkv[...] = jnp.sum(dqkv[...].astype(F32), axis=0, keepdims=True)

            def term_qkv(t, carry):
                flip[...] = act1[:, lanes(t, 256)].T
                term[...] = dot_nn(flip[...], dqkv[...]).reshape(R, rows, 3 * QB)
                at = pl.ds(pl.multiple_of(t * rows, rows), rows)

                def one_j(j, carry):
                    keep[j, at, : 3 * QB] = term[br[1] ^ (2 * j)]
                    send[j, at, : 3 * QB] = term[br[1] ^ (2 * j + 1)].astype(BF)
                    return carry

                return lax.fori_loop(0, J, one_j, carry, unroll=True)

            lax.fori_loop(0, NB, term_qkv, 0, unroll=True)

        grad_r, dqkv, keep_a, send_a, sum_qkv = call(
            bwd2_body,
            [("s", br), ("v", live)] + [("v", g) for g in grads_in]
            + [("v", a) for a in (hidden, mixed, act1, q, k, v, probs, cosine, sines, full_o)],
            [tab, sds((NT, 3 * QB), BF), sds((J, MF, D), F32), sds((J, MF, D), BF), sds((1, 3 * QB), F32)],
            [pltpu.VMEM((NT, QB), BF), pltpu.VMEM((R, rows, 3 * QB), F32), pltpu.VMEM((R, rows, D), F32), pltpu.VMEM((R, ff_dev, D), F32),
             pltpu.VMEM((256, NT), BF)],
            flops=2 * NT * D * (3 * QB + 2 * QB + FB) + 16 * NT * T * QB,
        )

        def bwd1_body(br, grad, act2, dgelu, wout, *rest):
            dhid, keep, send, sum_in, term_r, flip = rest

            def d_hidden(t, carry):
                cols = lanes(t, 256)
                per = 256 // ff_dev
                wt = wout[pl.ds(t * per, per)].reshape(256, D)
                y = (dot_nt(grad[...], wt) * dgelu[:, cols]).astype(BF)
                dhid[:, cols] = y
                sum_in[:, cols] = jnp.sum(y.astype(F32), axis=0, keepdims=True)
                return carry

            lax.fori_loop(0, FB // 256, d_hidden, 0, unroll=True)

            def term_in(t, carry):
                flip[...] = act2[:, lanes(t, 256)].T
                term_r[...] = dot_nn(flip[...], dhid[...]).reshape(R, rows, D)
                at = pl.ds(pl.multiple_of(t * rows, rows), rows)

                def one_j(j, carry):
                    keep[j, at] = term_r[br[1] ^ (2 * j)]
                    send[j, at] = term_r[br[1] ^ (2 * j + 1)].astype(BF)
                    return carry

                return lax.fori_loop(0, J, one_j, carry, unroll=True)

            lax.fori_loop(0, NB, term_in, 0, unroll=True)

        dhid, keep_f, send_f, sum_in = call(
            bwd1_body,
            [("s", br)] + [("v", a) for a in (grad_r, act2, dgelu, full_out)],
            [sds((NT, FB), BF), sds((J, MA, D), F32), sds((J, MA, D), BF), sds((1, FB), F32)],
            [pltpu.VMEM((R, rows, D), F32), pltpu.VMEM((256, NT), BF)],
            flops=4 * NT * D * FB,
        )

        def merge_body(keep, got, *outs):
            for j in range(J):
                y = keep[j] + got[j].astype(F32)
                outs[j][...] = y if j == 0 else y.astype(BF)

        def merge_small_body(keep, got, keep_small, got_small, *outs):
            for j in range(J):
                y = keep[j] + got[j].astype(F32)
                z = keep_small[j] + got_small[j].astype(F32)
                outs[j][:MA] = y.astype(outs[j].dtype)
                outs[j][MA:, :WO] = z.astype(outs[j].dtype)

        def merge(keep, send, small=()):
            size = keep.shape[1] + (8 if small else 0)
            ins = [keep, swap(send, 1), *small]
            outs = call(
                merge_small_body if small else merge_body, [("v", a) for a in ins],
                [sds((size, D), F32)] + [sds((size, D), BF)] * (J - 1),
            )
            return [outs[0]] + [swap(outs[j], 2 * j) for j in range(1, J)]

        if R == 8:

            def halves_body(keep, got, own, to_x, to_y, keep_x, keep_y):
                own[...] = keep[0] + got[0].astype(F32)
                low, high = slice(0, MA), slice(MA, MF)
                to_x[:MA] = (keep[1, low] + got[1, low].astype(F32)).astype(BF)
                to_x[MA:] = (keep[3, low] + got[3, low].astype(F32)).astype(BF)
                to_y[: MF - MA] = (keep[2, high] + got[2, high].astype(F32)).astype(BF)
                to_y[MF - MA :] = (keep[3, high] + got[3, high].astype(F32)).astype(BF)
                keep_x[...] = keep[1, high] + got[1, high].astype(F32)
                keep_y[...] = keep[2, low] + got[2, low].astype(F32)

            assert MF == 2 * MA
            quarter = sds((MA, D), F32)
            own_a, to_x, to_y, keep_x, keep_y = call(
                halves_body, [("v", keep_a), ("v", swap(send_a, 1))],
                [sds((MF, D), F32), sds((MF, D), BF), sds((MF, D), BF), quarter, quarter],
            )
            got_x, got_y = swap(to_x, 2), swap(to_y, 4)

            def second_body(keep_x, keep_y, got_x, got_y, to_x, to_y):
                to_x[...] = (keep_x[...] + got_y[MA:].astype(F32)).astype(BF)
                to_y[...] = (keep_y[...] + got_x[MA:].astype(F32)).astype(BF)

            to_x, to_y = call(
                second_body, [("v", a) for a in (keep_x, keep_y, got_x, got_y)],
                [sds((MA, D), BF), sds((MA, D), BF)],
            )
            merged_a = [own_a, got_x, got_y, swap(to_x, 2), swap(to_y, 4)]
            lower, upper = ((0, 0), (1, 0), (4, 0)), ((0, MA), (2, 0), (3, 0))
        else:
            merged_a = merge(keep_a, send_a)
            lower, upper = [(j, 0) for j in range(J)], [(j, MA) for j in range(J)]
        (pass_part,) = call(pass_body, [("v", later_part), ("v", got_one)], [block])
        got_two = across(pass_part, 2)

        out_widths = [FB * NB // n, 3 * D // n] + [D // n] * 5
        out_offsets = [sum(out_widths[:i]) for i in range(len(out_widths))]
        WO = -(-sum(out_widths) // 128) * 128

        def bwd3_body(br, xhat, w1, dqkv, dhid, grad, sum_in, sum_qkv, g1, g2, *rest):
            own, keep, send, *rest = rest
            aways, stages, (gs, sums, tot, semp) = rest[:3], rest[3:6], rest[6:]
            gs[...] = jnp.sum(grad[:T].astype(F32), axis=0, keepdims=True)

            def back(t, carry):
                cols = lanes(t, QB)
                d1 = dot_nt(dqkv[...], w1[t, :, :, : 3 * QB].reshape(QB, 3 * QB))
                d2 = dot_nt(dhid[...], w1[t, :, :, 3 * QB :].reshape(QB, FB))
                xh = xhat[:, cols]
                y = d1 * g1[:, cols] + d2 * g2[:, cols]
                own[:, cols] = y[:T]
                for k in range(1, NB):
                    stages[k - 1][:, cols] = y[k * T : (k + 1) * T].astype(BF)
                for i, z in enumerate((d1 * xh, d1, d2 * xh, d2)):
                    sums[i : i + 1, cols] = jnp.sum(z, axis=0, keepdims=True)
                return carry

            lax.fori_loop(0, D // QB, back, 0, unroll=True)
            sending = [pltpu.make_async_copy(a, z, semp.at[i]) for i, (a, z) in enumerate(zip(stages, aways))]
            for c in sending:
                c.start()

            total = jnp.zeros((n, WO), F32)

            def place(total, vec, col, which):
                size = vec.shape[1]
                width, off = out_widths[which], out_offsets[which]
                mine = jnp.where(iota((n, size), 0) == lax.div(col, width), vec, 0.0)
                base = off // 128 * 128
                span = -(-(off + width) // 128) * 128 - base
                sel = pick(lax.rem(col, width), off, base, span)
                high = mine.astype(BF)
                low = (mine - high.astype(F32)).astype(BF)
                placed = dot_nt(high, sel) + dot_nt(low, sel)
                parts = []
                if base:
                    parts.append(jnp.zeros((n, base), F32))
                parts.append(placed)
                if base + span < WO:
                    parts.append(jnp.zeros((n, WO - base - span), F32))
                return total + (jnp.concatenate(parts, axis=1) if len(parts) > 1 else placed)

            whole = iota((1, D), 1)
            at = iota((1, 3 * QB), 1)
            total = place(total, sum_in[...], iota((1, FB), 1) + br[0] * FB, 0)
            total = place(total, sum_qkv[...], lax.div(at, QB) * D + br[0] * QB + lax.rem(at, QB), 1)
            total = place(total, gs[...], whole, 2)
            for i in range(4):
                total = place(total, sums[i : i + 1], whole, 3 + i)
            tot[...] = total
            for j in range(J):
                for ref, m in ((keep, 2 * j), (send, 2 * j + 1)):
                    lines = [tot[pl.ds(to * R + (br[1] ^ m), 1), :] for to in range(NB)]
                    lines.append(jnp.zeros((8 - NB, WO), F32))
                    ref[j] = jnp.concatenate(lines, axis=0).astype(ref.dtype)
            for c in sending:
                c.wait()

        own_g, keep_s, send_s, *away_g = call(
            bwd3_body,
            [("s", br)] + [("v", a) for a in (xhat, full_one, dqkv, dhid, grad_r, sum_in, sum_qkv, gain_one, gain_two)],
            [sds((T, D), F32), sds((J, 8, WO), F32), sds((J, 8, WO), BF), block, block, block],
            [pltpu.VMEM((T, D), BF)] * 3 + [pltpu.VMEM((1, D), F32), pltpu.VMEM((8, D), F32), pltpu.VMEM((n, WO), F32), dma((3,))],
            hbm=(3, 4, 5),
            flops=2 * NT * D * W1,
        )
        backs = [across(g, k + 1) for k, g in enumerate(away_g)]
        merged_f = merge(keep_f, send_f, (keep_s, swap(send_s, 1)))

        def total_body(x, live_ref, bo, own, p1, p2, out):
            def fn(rws):
                y = x[rws].astype(F32) + bo[...] + own[rws] + p1[rws].astype(F32) + p2[rws].astype(F32)
                out[rws] = (y * live_ref[rws]).astype(BF)

            by_rows(T, T, fn)

        (block_out,) = call(
            total_body,
            [("v", a) for a in (block_in, live[:T], bias_o, own_part, got_one, got_two)], [block],
        )

        def plane_f_body(br, *rest):
            got, (z0, z1, z2, z3) = rest[:J], rest[J:]

            def total_of(at, low, high):
                y = got[0][at, low:high]
                for ref in got[1:]:
                    y = y + ref[at, low:high].astype(F32)
                return y

            lines = total_of(slice(MA, MS), 0, WO)
            for k, ref in enumerate((z0, z1, z2, z3)):
                at = pl.ds(pl.multiple_of((br[0] ^ k) * rows, rows), rows)
                ref[:rows] = total_of(at, 0, FB).astype(ref.dtype)
                y = jnp.sum(jnp.where(iota(lines.shape, 0) == (br[0] ^ k), lines, 0.0), axis=0, keepdims=True)
                ref[rows:, :WO] = jnp.broadcast_to(y, (8, WO)).astype(ref.dtype)

        zf0, *zf = call(
            plane_f_body, [("s", br)] + [("v", a) for a in merged_f],
            [sds((rows + 8, FB), F32)] + [sds((rows + 8, FB), BF)] * 3,
        )

        def plane_a_body(br, *rest):
            got, (w_o_ref, w_out_ref, z0, z1, z2, z3) = rest[: len(merged_a)], rest[len(merged_a) :]

            def total_of(part, start, size, low, high):
                y = 0.0
                for which, first in part:
                    at = first + start
                    if not isinstance(at, int):
                        at = pl.multiple_of(at, 8)
                    y = y + got[which][pl.ds(at, size), low:high].astype(F32)
                return y

            w_out_ref[...] = total_of(upper, 0, ff_dev, 0, D)
            for c in range(NB):
                w_o_ref[:, c * QB : (c + 1) * QB] = total_of(lower, c * rows, rows, 3 * QB, D)
            for k, ref in enumerate((z0, z1, z2, z3)):
                ref[...] = total_of(lower, (br[0] ^ k) * rows, rows, 0, 3 * QB).astype(ref.dtype)

        grad_w_o, grad_w_out, za0, *za = call(
            plane_a_body, [("s", br)] + [("v", a) for a in merged_a],
            [sds((rows, D), F32), sds((ff_dev, D), F32), sds((rows, 3 * QB), F32)] + [sds((rows, 3 * QB), BF)] * 3,
        )
        zf = [zf0] + [across(z, k + 1) for k, z in enumerate(zf)]
        za = [za0] + [across(z, k + 1) for k, z in enumerate(za)]

        small_order = (0, 1, 2, 2, 3, 4, 5, 6)

        def place_f_body(br, z0, z1, z2, z3, out, *small):
            y = sum(ref[rows:, :WO].astype(F32) for ref in (z0, z1, z2, z3))
            for ref, which in zip(small, small_order):
                ref[...] = y[:1, out_offsets[which] : out_offsets[which] + out_widths[which]]
            for k, ref in enumerate((z0, z1, z2, z3)):
                out[:, lanes(br[0] ^ k, FB)] = ref[:rows].astype(F32)

        def place_a_body(br, z0, z1, z2, z3, out):
            for k, ref in enumerate((z0, z1, z2, z3)):
                at = br[0] ^ k
                for s in range(3):
                    out[:, lanes(s * NB + at, QB)] = ref[:, s * QB : (s + 1) * QB].astype(F32)

        def input_body(x, grad, own, p1, p2, p3, out):
            def fn(rws):
                centered, rstd = stats(x[rws].astype(F32))
                xh = centered * rstd
                g = own[rws] + p1[rws].astype(F32) + p2[rws].astype(F32) + p3[rws].astype(F32)
                mean_g = jnp.mean(g, axis=-1, keepdims=True)
                mean_gx = jnp.mean(g * xh, axis=-1, keepdims=True)
                out[rws] = (grad[rws].astype(F32) + rstd * (g - mean_g - xh * mean_gx)).astype(BF)

            by_rows(T, T, fn)

        def final_body(br, *rest):
            ins, outs = rest[:14], rest[14:]
            place_f_body(br, *ins[6:10], outs[1], *outs[3:])
            place_a_body(br, *ins[10:14], outs[2])
            input_body(*ins[:6], outs[0])

        grad_input, grad_w_in, grad_w_qkv, *outs = call(
            final_body,
            [("s", br)] + [("v", a) for a in (block_in, grad_r[:T], own_g, *backs, *zf, *za)],
            [block, sds((rows, NB * FB), F32), sds((rows, 3 * D), F32)] + [sds((1, out_widths[i]), F32) for i in small_order],
        )
        outs = [o.reshape(-1) for o in outs]

        grad_b_in, grad_b_qkv, grad_b_o, grad_b_out, grad_g1, grad_s1, grad_g2, grad_s2 = outs
        return (
            block_out, grad_input, grad_w_qkv, grad_b_qkv, grad_w_o, grad_b_o, grad_w_in, grad_b_in,
            grad_w_out, grad_b_out, grad_g1, grad_s1, grad_g2, grad_s2,
        )

    return on_device


def solution(mesh):
    two, one = P("dp", None), P("dp")
    n = mesh.shape["dp"]
    on_device = make(n)

    return jax.shard_map(
        on_device,
        mesh=mesh,
        in_specs=(two, two, two, one, two, one, two, one, two, one, one, one, one, one, P(), P(), P()),
        out_specs=(two, two, two, one, two, one, two, one, two, one, one, one, one, one),
        check_vma=False,
    )
```

```python
import math

import jax
import jax.numpy as jnp
from jax import lax
from jax.experimental import pallas as pl
from jax.experimental.pallas import tpu as pltpu
from jax.sharding import PartitionSpec as P


D = 1024
HEAD = 64
ROT = 16
NB = 4
QB = D // NB
NEG = -1e30
SHARE = 1.0
TWO_STEPS = True
HALVES = False

F32 = jnp.float32
BF = jnp.bfloat16
I32 = jnp.int32


def dot_nn(left, right):
    return jnp.dot(left, right, preferred_element_type=F32)


def dot_nt(left, right):
    return lax.dot_general(left, right, (((1,), (1,)), ((), ())), preferred_element_type=F32)


def iota(shape, axis):
    return lax.broadcasted_iota(I32, shape, axis)


def call(body, ins, outs, scratch=(), flops=0, extra=4 << 20, hbm=(), alias=None):
    spaces = {"v": pltpu.VMEM, "s": pltpu.SMEM, "a": pl.ANY, "h": pltpu.HBM}
    arrays = [a for _, a in ins]
    nbytes = sum(a.size * a.dtype.itemsize for a in arrays) + sum(math.prod(o.shape) * o.dtype.itemsize for o in outs)
    room = sum(math.prod(t.shape) * jnp.dtype(t.dtype).itemsize for t in scratch if getattr(t, "memory_space", None) == pltpu.VMEM)
    room += SHARE * (sum(a.size * a.dtype.itemsize for s, a in ins if s == "v") + sum(math.prod(o.shape) * o.dtype.itemsize for i, o in enumerate(outs) if i not in hbm))
    return pl.pallas_call(
        body,
        out_shape=tuple(outs),
        in_specs=[pl.BlockSpec(memory_space=spaces[s]) for s, _ in ins],
        out_specs=tuple(pl.BlockSpec(memory_space=pltpu.HBM if i in hbm else pltpu.VMEM) for i in range(len(outs))),
        scratch_shapes=list(scratch),
        input_output_aliases=alias or {},
        compiler_params=pltpu.CompilerParams(vmem_limit_bytes=int(room * 1.02) + extra),
        cost_estimate=pl.CostEstimate(flops=int(flops), bytes_accessed=int(nbytes), transcendentals=0),
    )(*arrays)


def sds(shape, dtype):
    return jax.ShapeDtypeStruct(shape, dtype)


def by_rows(count, chunk, fn):
    def step(i, carry):
        fn(pl.ds(pl.multiple_of(i * chunk, chunk), chunk))
        return carry

    lax.fori_loop(0, count // chunk, step, 0, unroll=True)


def lanes(i, width):
    return pl.ds(pl.multiple_of(i * width, width), width)


def partner(v):
    low = iota(v.shape, 1) % HEAD < ROT // 2
    return jnp.where(low, pltpu.roll(v, v.shape[1] - ROT // 2, 1), pltpu.roll(v, ROT // 2, 1))


def split_heads(v):
    first = iota(v.shape, 1) < HEAD
    zero = jnp.zeros_like(v)
    return jnp.concatenate([jnp.where(first, v, zero), jnp.where(first, zero, v)], axis=0)


def stats(x):
    centre = jnp.mean(x, axis=-1, keepdims=True)
    centered = x - centre
    spread = jnp.mean(centered * centered, axis=-1, keepdims=True)
    return centered, lax.rsqrt(spread + 1e-05)


def make(n):
    R = n // NB
    assert R * NB == n and R & (R - 1) == 0

    def across(v, mask):
        return lax.ppermute(v, "dp", [(d, d ^ (mask * R)) for d in range(n)])

    def swap(v, mask):
        return lax.ppermute(v, "dp", [(d, d ^ mask) for d in range(n)])

    def gather_r(own, tag):
        half = own.shape[0] // 2
        got = [(0, 0, own)]
        if R == 8 and tag == "one":
            from_x, from_y = swap(own, 2), swap(own, 4)
            got += [(2, 0, from_x), (4, 0, from_y)]


            def cut_body(x, y, low, high):
                low[...] = y[:half]
                high[...] = x[half:]

            part = sds((half, *own.shape[1:]), BF)
            low, high = call(cut_body, [("v", from_x), ("v", from_y)], [part, part])
            got.append((6, 0, swap(low, 2)))
            got.append((6, half, swap(high, 4)))
        else:
            for m in range(2, R, 2):
                got.append((m, 0, swap(own, m)))
        return got + [(m + 1, at, swap(v, 1)) for m, at, v in got]

    def on_device(
        block_in, grad_out, w_qkv, b_qkv, w_o, b_o, w_in, b_in, w_out, b_out,
        ln1_gain, ln1_shift, ln2_gain, ln2_shift, seq_lens, seq_device, seq_offset,
    ):
        T = block_in.shape[0]
        NT = NB * T
        rows = w_qkv.shape[0]
        ff_dev = w_out.shape[0]
        FB = w_in.shape[1] // NB
        W1 = 3 * QB + FB
        J = R // 2
        MA = NB * rows
        MS = MA + 8
        idx = lax.axis_index("dp").astype(I32)
        b, r = idx // R, idx % R
        br = jnp.stack([b, r])

        count = seq_lens.shape[0]
        half = ROT // 2

        def table_body(br, lens, device, offset, cos, sin, mask, live):
            slot = iota((T, count), 0)
            lane = iota((T, 2 * HEAD), 1) % HEAD
            freqs = jnp.exp((lane % half).astype(F32) * (-math.log(10000.0) / half))
            freqs = jnp.where(lane < ROT, freqs, 0.0)
            causal = iota((T, T), 1) <= iota((T, T), 0)
            for k in range(NB):
                owner = (br[0] ^ k) * R + br[1]
                inside = (device[...] == owner) & (slot >= offset[...]) & (slot < offset[...] + lens[...])
                ones = jnp.where(inside, 1.0, 0.0)
                present = jnp.max(ones, axis=1, keepdims=True)
                number = jnp.sum(ones * iota((T, count), 1).astype(F32), axis=1, keepdims=True)
                position = jnp.sum(ones * (slot - offset[...]).astype(F32), axis=1, keepdims=True)
                own = (count + iota((T, 1), 0)).astype(F32)
                segment = jnp.broadcast_to(jnp.where(present > 0.0, number, own), (T, T))
                mask[k] = jnp.where((segment == segment.T) & causal, 0.0, NEG)
                rws = slice(k * T, (k + 1) * T)
                live[rws] = present
                angle = position * freqs
                cos[rws] = jnp.cos(angle)
                sin[rws] = jnp.sin(angle) * jnp.where(lane < half, -1.0, 1.0)

        table = sds((NT, 2 * HEAD), F32)
        cosine, sines, mask, live = call(
            table_body, [("s", br)] + [("v", v.reshape(1, -1)) for v in (seq_lens, seq_device, seq_offset)],
            [table, table, sds((NB, T, T), F32), sds((NT, 1), F32)],
        )

        small = [b_in, b_qkv, b_o, b_out, ln1_gain, ln1_shift, ln2_gain, ln2_shift]
        widths = [v.shape[0] for v in small]
        offsets = [sum(widths[:i]) for i in range(len(small))]
        SR = -(-sum(widths) // 128)
        W1X = W1 + 128

        def pack_body(qkv_ref, in_ref, o_ref, out_ref, *rest):
            vectors, outs = rest[: len(small)], rest[len(small) :]
            for k in range(NB):
                to = lax.div(lax.axis_index("dp").astype(I32), R) ^ k
                for s in range(3):
                    outs[k][:, s * QB : (s + 1) * QB] = qkv_ref[:, lanes(s * NB + to, QB)]
                outs[k][:, 3 * QB : W1] = in_ref[:, lanes(to, FB)]
            outs[NB][:ff_dev] = out_ref[...]
            outs[NB][ff_dev:] = o_ref[...]
            parts = [v[...].astype(F32) for v in vectors]
            if SR * 128 > sum(widths):
                parts.append(jnp.zeros((1, SR * 128 - sum(widths)), F32))
            every = jnp.concatenate(parts, axis=1)
            lines = [every[:, i * 128 : (i + 1) * 128] for i in range(SR)]
            if rows > SR:
                lines.append(jnp.zeros((rows - SR, 128), F32))
            lines = jnp.concatenate(lines, axis=0).astype(BF)
            for k in range(NB):
                outs[k][:, W1:] = lines

        packed = call(
            pack_body,
            [("v", w_qkv), ("v", w_in), ("v", w_o), ("v", w_out)] + [("v", v.reshape(1, -1)) for v in small],
            [sds((rows, W1X), BF)] * NB + [sds((ff_dev + rows, D), BF)], extra=56 << 20,
        )
        columns, own_two = packed[:NB], packed[NB]

        def blocks_of(own, after):
            two = across(after, 2)
            return [own, across(after, 1), two, across(two, 1)]

        two = gather_r(own_two, "two")
        crossed = [across(columns[k], k) for k in range(1, NB)]
        after, _ = lax.optimization_barrier((block_in, crossed))

        def join_body(*refs):
            for k in range(NB):
                refs[NB][k] = refs[k][...]

        (mine,) = call(join_body, [("v", a) for a in (columns[0], *crossed)], [sds((NB, rows, W1X), BF)])
        one = gather_r(mine, "one")
        tokens = blocks_of(block_in, after)
        after, _ = lax.optimization_barrier((grad_out, tokens[1]))
        grads_in = [grad_out] + [across(after, k) for k in range(1, NB)]

        def pick(width_mod, off, base, width):
            return (iota((width, width_mod.shape[1]), 0) + base == off + width_mod).astype(BF)

        def window(off, width):
            base = off // 128 * 128
            return base, -(-(off + width) // 128) * 128 - base

        def decode(br, got, bq, bi, g1, s1, g2, s2, bo):
            def expand(which, col):
                width, off = widths[which], offsets[which]
                base, span = window(off, width)
                total = col.shape[1]
                sel = pick(lax.rem(col, width), off, base, span)
                every = dot_nn(jnp.concatenate([got[:, i] for i in range(base // 128, (base + span) // 128)], axis=1), sel)
                return jnp.sum(jnp.where(iota((n, total), 0) == lax.div(col, width), every, 0.0), axis=0, keepdims=True)

            at = iota((1, 3 * QB), 1)
            bq[...] = expand(1, lax.div(at, QB) * D + br[0] * QB + lax.rem(at, QB))
            bi[...] = expand(0, iota((1, FB), 1) + br[0] * FB)
            whole = iota((1, D), 1)
            bo[...] = expand(2, whole) + expand(3, whole)
            for ref, which in ((g1, 4), (s1, 5), (g2, 6), (s2, 7)):
                ref[...] = expand(which, whole)

        def load_small(br, parts, got, sems):
            copies = []
            for (m, start, _), ref in zip(one, parts):
                for k in range(ref.shape[0]):
                    at = (br[0] ^ (start + k)) * R + (br[1] ^ m)
                    source = ref.at[k, pl.ds(0, 8), pl.ds(W1, 128)]
                    copies.append(pltpu.make_async_copy(source, got.at[at], sems.at[len(copies)]))
            return copies

        def load_one(br, parts, w1, sems, low, high):
            cols = pl.ds(low, high - low)
            copies = []
            for (m, start, _), ref in zip(one, parts):
                for k in range(ref.shape[0]):
                    to = w1.at[br[0] ^ (start + k), br[1] ^ m, :, cols]
                    copies.append(pltpu.make_async_copy(ref.at[k, :, cols], to, sems.at[int(low > 0), len(copies)]))
            return copies

        def load_two(br, parts, wout, wo, sems):
            copies = []
            for (m, start, _), ref in zip(two, parts):
                size = ref.shape[0]
                for to, first, last in ((wout, 0, ff_dev), (wo, ff_dev, ff_dev + rows)):
                    low, high = max(start, first), min(start + size, last)
                    if low < high:
                        copies.append(
                            pltpu.make_async_copy(
                                ref.at[pl.ds(low - start, high - low)],
                                to.at[br[1] ^ m, pl.ds(low - first, high - low)],
                                sems.at[len(copies)],
                            )
                        )
            return copies

        dma = pltpu.SemaphoreType.DMA
        PAIRS = QB // 128

        def fwd_body(br, h0, h1, h2, h3, cos, sin, mask_ref, *rest):
            one_refs, two_refs, rest = rest[: len(one)], rest[len(one) : len(one) + len(two)], rest[len(one) + len(two) :]
            act1, act2, q, k, v, probs, mixed, hidden, dgelu, xhat_ref, w1, wo, wout, own, later, away = rest[:16]
            g1, g2, bo = rest[16:19]
            stage, x_ref, semx, sem1, sem2, semp, bq, bi, s1, s2, got, semg = rest[19:]
            cx = [pltpu.make_async_copy(h, x_ref.at[i], semx.at[i]) for i, h in enumerate((h0, h1, h2, h3))]
            c1, c1f = load_one(br, one_refs, w1, sem1, 0, 3 * QB), load_one(br, one_refs, w1, sem1, 3 * QB, W1)
            c2, cg = load_two(br, two_refs, wout, wo, sem2), load_small(br, one_refs, got, semg)
            for c in cx + cg + c1 + c1f + c2:
                c.start()
            for i in range(NB):
                cx[i].wait()
                centered, rstd = stats(x_ref[i].astype(F32))
                xhat_ref[i * T : (i + 1) * T] = centered * rstd
            for c in cg:
                c.wait()
            decode(br, got, bq, bi, g1, s1, g2, s2, bo)
            for i in range(NB):
                rws = slice(i * T, (i + 1) * T)
                act1[rws] = (xhat_ref[rws] * g1[...] + s1[...]).astype(BF)
                act2[rws] = (xhat_ref[rws] * g2[...] + s2[...]).astype(BF)
            for c in c1:
                c.wait()
            for s, ref in enumerate((q, k, v)):
                wt = w1[:, :, :, s * QB : (s + 1) * QB].reshape(D, QB)

                def project(rws, s=s, ref=ref, wt=wt):
                    y = dot_nn(act1[rws], wt) + bq[:, s * QB : (s + 1) * QB]
                    for p in range(PAIRS):
                        z = y[:, p * 128 : (p + 1) * 128]
                        if s < 2:
                            z = z * cos[rws] + partner(z) * sin[rws]
                        ref[rws, p * 128 : (p + 1) * 128] = z.astype(BF)

                by_rows(NT, 256, project)

            def attend(i, carry):
                rws = pl.ds(pl.multiple_of(i * T, T), T)
                m2 = mask_ref[i]
                m2 = jnp.concatenate([m2, m2], axis=0)
                for p in range(PAIRS):
                    cols = slice(p * 128, (p + 1) * 128)
                    s = dot_nt(split_heads(q[rws, cols]), k[rws, cols]) * (1.0 / math.sqrt(HEAD)) + m2
                    e = jnp.exp(s - jnp.max(s, axis=-1, keepdims=True))
                    pr = e / jnp.sum(e, axis=-1, keepdims=True)
                    probs[i * PAIRS + p] = pr
                    pb = pr.astype(BF)
                    pb = jnp.concatenate([pb[:T], pb[T:]], axis=1)
                    mixed[rws, cols] = dot_nn(pb, split_heads(v[rws, cols])).astype(BF)
                return carry

            lax.fori_loop(0, NB, attend, 0, unroll=True)
            for c in c1f:
                c.wait()

            def feed(t, carry):
                cols = lanes(t, 256)
                wt = w1[:, :, :, pl.ds(pl.multiple_of(3 * QB + t * 256, 256), 256)].reshape(D, 256)

                def act(rws):
                    h = dot_nn(act2[rws], wt) + bi[:, cols]
                    cdf = 0.5 * (1.0 + lax.erf(h * (1.0 / math.sqrt(2.0))))
                    hidden[rws, cols] = (h * cdf).astype(BF)
                    dgelu[rws, cols] = cdf + h * (jnp.exp(-0.5 * h * h) * (1.0 / math.sqrt(2.0 * math.pi)))

                by_rows(NT, 256, act)
                return carry

            lax.fori_loop(0, FB // 256, feed, 0, unroll=True)
            for c in c2:
                c.wait()

            def project_out(t, carry):
                cols = lanes(t, 256)
                y = dot_nn(mixed[...], wo[:, :, cols].reshape(QB, 256))
                y = y + dot_nn(hidden[...], wout[:, :, cols].reshape(FB, 256))
                own[:, cols] = y[:T]
                later[:, cols] = y[2 * T : 3 * T]
                stage[:T, cols] = y[T : 2 * T].astype(BF)
                stage[T:, cols] = y[3 * T :].astype(BF)
                return carry

            lax.fori_loop(0, D // 256, project_out, 0, unroll=True)
            send = pltpu.make_async_copy(stage, away, semp)
            send.start()
            send.wait()

        tab = sds((NT, D), BF)
        third = sds((NT, QB), BF)
        block = sds((T, D), BF)
        act1, act2, q, k, v, probs, mixed, hidden, dgelu, xhat, full_one, full_o, full_out, own_part, later_part, away_part, gain_one, gain_two, bias_o = call(
            fwd_body,
            [("s", br)] + [("h", x) for x in tokens]
            + [("v", a) for a in (cosine, sines, mask)]
            + [("h", a) for _, _, a in one + two],
            [tab, tab, third, third, third, sds((NB * PAIRS, 2 * T, T), F32), third, sds((NT, FB), BF), sds((NT, FB), F32),
             sds((NT, D), F32), sds((NB, R, rows, W1), BF), sds((R, rows, D), BF), sds((R, ff_dev, D), BF),
             sds((T, D), F32), sds((T, D), F32), sds((2 * T, D), BF)] + [sds((1, D), F32)] * 3,
            [pltpu.VMEM((2 * T, D), BF), pltpu.VMEM((NB, T, D), BF), dma((NB,)), dma((2, R * NB)), dma((3 * R,)), dma,
             pltpu.VMEM((1, 3 * QB), F32), pltpu.VMEM((1, FB), F32), pltpu.VMEM((1, D), F32), pltpu.VMEM((1, D), F32),
             pltpu.VMEM((n, 8, 128), BF), dma((R * NB,))],
            hbm=(15,),
            flops=2 * NT * D * W1 + 2 * NT * D * (QB + FB) + 8 * NT * T * QB,
        )

        got_one = across(away_part, 1)

        def pass_body(keep, got, out):
            def fn(rws):
                out[rws] = (keep[rws] + got[pl.ds(T, T)].astype(F32)).astype(BF)

            by_rows(T, T, fn)


        def bwd_core_body(br, live_ref, g0, g1, g2, g3, act1, act2, q, k, v, probs, cos, sin, dgelu, wo, wout, *rest):
            grad, dqkv, dhid, keep, send, sum_qkv, sum_in, dmix, term, flip = rest
            for i, g in enumerate((g0, g1, g2, g3)):
                rws = pl.ds(i * T, T)
                grad[rws] = (g[...].astype(F32) * live_ref[rws]).astype(BF)
            dmix[...] = dot_nt(grad[...], wo[...].reshape(QB, D)).astype(BF)

            def attend(i, carry):
                rws = pl.ds(pl.multiple_of(i * T, T), T)
                for p in range(PAIRS):
                    cols = slice(p * 128, (p + 1) * 128)
                    pr = probs[i * PAIRS + p]
                    pb = pr.astype(BF)
                    dm2 = split_heads(dmix[rws, cols])
                    dp = dot_nt(dm2, v[rws, cols])
                    ds = (pr * (dp - jnp.sum(dp * pr, axis=-1, keepdims=True))).astype(BF)
                    dq = dot_nn(jnp.concatenate([ds[:T], ds[T:]], axis=1), split_heads(k[rws, cols]))
                    dk = dot_nn(ds.T, split_heads(q[rws, cols]))
                    dv = dot_nn(pb.T, dm2)
                    for s, z in enumerate((dq, dk)):
                        z = z * (1.0 / math.sqrt(HEAD))
                        z = z * cos[rws] - partner(z) * sin[rws]
                        dqkv[rws, s * QB + p * 128 : s * QB + (p + 1) * 128] = z.astype(BF)
                    dqkv[rws, 2 * QB + p * 128 : 2 * QB + (p + 1) * 128] = dv.astype(BF)
                return carry

            lax.fori_loop(0, NB, attend, 0, unroll=True)
            sum_qkv[...] = jnp.sum(dqkv[...].astype(F32), axis=0, keepdims=True)

            def d_hidden(t, carry):
                cols = lanes(t, 256)
                per = 256 // ff_dev
                wt = wout[pl.ds(t * per, per)].reshape(256, D)
                y = (dot_nt(grad[...], wt) * dgelu[:, cols]).astype(BF)
                dhid[:, cols] = y
                sum_in[:, cols] = jnp.sum(y.astype(F32), axis=0, keepdims=True)
                return carry

            lax.fori_loop(0, FB // 256, d_hidden, 0, unroll=True)

            def terms(t, carry):
                cols = lanes(t, 256)
                flip[0] = act1[:, cols].T
                flip[1] = act2[:, cols].T
                term[:, :, : 3 * QB] = dot_nn(flip[0], dqkv[...]).reshape(R, rows, 3 * QB)
                term[:, :, 3 * QB :] = dot_nn(flip[1], dhid[...]).reshape(R, rows, FB)
                at = pl.ds(pl.multiple_of(t * rows, rows), rows)
                for j in range(J):
                    keep[j, at] = term[br[1] ^ (2 * j)]
                    send[j, at] = term[br[1] ^ (2 * j + 1)].astype(BF)
                return carry

            lax.fori_loop(0, NB, terms, 0, unroll=True)

        grad_r, dqkv, dhid, keep_1, send_1, sum_qkv, sum_in = call(
            bwd_core_body,
            [("s", br), ("v", live)] + [("v", g) for g in grads_in]
            + [("v", a) for a in (act1, act2, q, k, v, probs, cosine, sines, dgelu, full_o, full_out)],
            [tab, sds((NT, 3 * QB), BF), sds((NT, FB), BF), sds((J, MA, W1), F32), sds((J, MA, W1), BF),
             sds((1, 3 * QB), F32), sds((1, FB), F32)],
            [pltpu.VMEM((NT, QB), BF), pltpu.VMEM((R, rows, W1), F32), pltpu.VMEM((2, 256, NT), BF)],
            flops=2 * NT * D * (W1 + QB + FB) + 16 * NT * T * QB,
        )

        def merge(keep, send, small=()):
            size, width = keep.shape[1:]

            def body(keep, got, *rest):
                keep_small, got_small = rest[: len(small)] or (None, None)
                outs = rest[len(small) :]
                for j in range(J):
                    y = keep[j] + got[j].astype(F32)
                    outs[j][:size] = y.astype(outs[j].dtype)
                    if small:
                        z = keep_small[j] + got_small[j].astype(F32)
                        outs[j][size:, :WO] = z.astype(outs[j].dtype)

            full = size + (8 if small else 0)
            outs = call(
                body, [("v", a) for a in (keep, swap(send, 1), *small)],
                [sds((full, width), F32)] + [sds((full, width), BF)] * (J - 1),
            )
            return [outs[0]] + [swap(outs[j], 2 * j) for j in range(1, J)]

        (pass_part,) = call(pass_body, [("v", later_part), ("v", got_one)], [block])
        got_two = across(pass_part, 2)

        out_widths = [FB * NB // n, 3 * D // n] + [D // n] * 5
        out_offsets = [sum(out_widths[:i]) for i in range(len(out_widths))]
        WO = -(-sum(out_widths) // 128) * 128

        def bwd3_body(br, xhat, w1, dqkv, dhid, grad, sum_in, sum_qkv, g1, g2, *rest):
            own, keep, send, *rest = rest
            parts = 1 if TWO_STEPS else 3
            aways, rest = rest[:parts], rest[parts:]
            later, rest = (rest[:1], rest[1:]) if TWO_STEPS else ((), rest)
            stages, (gs, sums, tot, semp) = rest[:parts], rest[parts:]
            gs[...] = jnp.sum(grad[:T].astype(F32), axis=0, keepdims=True)

            def back(t, carry):
                cols = lanes(t, QB)
                d1 = dot_nt(dqkv[...], w1[t, :, :, : 3 * QB].reshape(QB, 3 * QB))
                d2 = dot_nt(dhid[...], w1[t, :, :, 3 * QB :].reshape(QB, FB))
                xh = xhat[:, cols]
                y = d1 * g1[:, cols] + d2 * g2[:, cols]
                own[:, cols] = y[:T]
                for k in range(1, NB):
                    if not TWO_STEPS:
                        stages[k - 1][:, cols] = y[k * T : (k + 1) * T].astype(BF)
                    elif k == 2:
                        later[0][:, cols] = y[k * T : (k + 1) * T]
                    else:
                        stages[0][(k // 2) * T : (k // 2 + 1) * T, cols] = y[k * T : (k + 1) * T].astype(BF)
                for i, z in enumerate((d1 * xh, d1, d2 * xh, d2)):
                    sums[i : i + 1, cols] = jnp.sum(z, axis=0, keepdims=True)
                return carry

            lax.fori_loop(0, D // QB, back, 0, unroll=True)
            sending = [pltpu.make_async_copy(a, z, semp.at[i]) for i, (a, z) in enumerate(zip(stages, aways))]
            for c in sending:
                c.start()

            total = jnp.zeros((n, WO), F32)

            def place(total, vec, col, which):
                size = vec.shape[1]
                width, off = out_widths[which], out_offsets[which]
                mine = jnp.where(iota((n, size), 0) == lax.div(col, width), vec, 0.0)
                base = off // 128 * 128
                span = -(-(off + width) // 128) * 128 - base
                sel = pick(lax.rem(col, width), off, base, span)
                high = mine.astype(BF)
                low = (mine - high.astype(F32)).astype(BF)
                placed = dot_nt(high, sel) + dot_nt(low, sel)
                parts = []
                if base:
                    parts.append(jnp.zeros((n, base), F32))
                parts.append(placed)
                if base + span < WO:
                    parts.append(jnp.zeros((n, WO - base - span), F32))
                return total + (jnp.concatenate(parts, axis=1) if len(parts) > 1 else placed)

            whole = iota((1, D), 1)
            at = iota((1, 3 * QB), 1)
            total = place(total, sum_in[...], iota((1, FB), 1) + br[0] * FB, 0)
            total = place(total, sum_qkv[...], lax.div(at, QB) * D + br[0] * QB + lax.rem(at, QB), 1)
            total = place(total, gs[...], whole, 2)
            for i in range(4):
                total = place(total, sums[i : i + 1], whole, 3 + i)
            tot[...] = total
            for j in range(J):
                for ref, m in ((keep, 2 * j), (send, 2 * j + 1)):
                    lines = [tot[pl.ds(to * R + (br[1] ^ m), 1), :] for to in range(NB)]
                    lines.append(jnp.zeros((8 - NB, WO), F32))
                    ref[j] = jnp.concatenate(lines, axis=0).astype(ref.dtype)
            for c in sending:
                c.wait()

        pair = sds((2 * T, D), BF)
        own_g, keep_s, send_s, *away_g = call(
            bwd3_body,
            [("s", br)] + [("v", a) for a in (xhat, full_one, dqkv, dhid, grad_r, sum_in, sum_qkv, gain_one, gain_two)],
            [sds((T, D), F32), sds((J, 8, WO), F32), sds((J, 8, WO), BF)]
            + ([pair, sds((T, D), F32)] if TWO_STEPS else [block] * 3),
            [pltpu.VMEM((2 * T, D) if TWO_STEPS else (T, D), BF)] * (1 if TWO_STEPS else 3)
            + [pltpu.VMEM((1, D), F32), pltpu.VMEM((8, D), F32), pltpu.VMEM((n, WO), F32), dma((3,))],
            hbm=(3,) if TWO_STEPS else (3, 4, 5), flops=2 * NT * D * W1,
        )
        if TWO_STEPS:
            back_one = across(away_g[0], 1)
            (pass_g,) = call(pass_body, [("v", away_g[1]), ("v", back_one)], [block])
            backs = [back_one, across(pass_g, 2)]
        else:
            backs = [across(g, k + 1) for k, g in enumerate(away_g)]
        HALF = MA // 2
        if R == 8 and HALVES:

            def halves_body(keep, got, keep_small, got_small, own, to_x, to_y, keep_x, keep_y):
                def total(j, low, high):
                    return keep[j, low:high] + got[j, low:high].astype(F32)

                def small(j):
                    return keep_small[j] + got_small[j].astype(F32)

                own[:MA] = total(0, 0, MA)
                own[MA:, :WO] = small(0)
                to_x[:HALF] = total(1, 0, HALF).astype(BF)
                to_x[HALF:] = total(3, 0, HALF).astype(BF)
                for at, j in ((0, 2), (MS - HALF, 3)):
                    to_y[at : at + MA - HALF] = total(j, HALF, MA).astype(BF)
                    to_y[at + MA - HALF : at + MS - HALF, :WO] = small(j).astype(BF)
                keep_x[: MA - HALF] = total(1, HALF, MA)
                keep_x[MA - HALF :, :WO] = small(1)
                keep_y[...] = total(2, 0, HALF)

            own_1, to_x, to_y, keep_x, keep_y = call(
                halves_body,
                [("v", a) for a in (keep_1, swap(send_1, 1), keep_s, swap(send_s, 1))],
                [sds((MS, W1), F32), sds((2 * HALF, W1), BF), sds((2 * (MS - HALF), W1), BF), sds((MS - HALF, W1), F32),
                 sds((HALF, W1), F32)],
            )
            got_x, got_y = swap(to_x, 2), swap(to_y, 4)

            def second_body(keep_x, keep_y, got_x, got_y, to_x, to_y):
                to_x[...] = (keep_x[...] + got_y[MS - HALF :].astype(F32)).astype(BF)
                to_y[...] = (keep_y[...] + got_x[HALF:].astype(F32)).astype(BF)

            to_x, to_y = call(
                second_body, [("v", a) for a in (keep_x, keep_y, got_x, got_y)],
                [sds((MS - HALF, W1), BF), sds((HALF, W1), BF)],
            )
            merged_1 = [own_1, got_x, got_y, swap(to_x, 2), swap(to_y, 4)]
            lower, upper = ((0, 0), (1, 0), (4, 0)), ((0, 0), (2, -HALF), (3, -HALF))
        else:
            merged_1 = merge(keep_1, send_1, (keep_s, swap(send_s, 1)))
            lower = upper = [(j, 0) for j in range(J)]

        def terms_body(br, grad, hidden, mixed, keep, send, term, term_o, flip):
            def term_out(t, carry):
                flip[...] = hidden[:, lanes(t, 256)].T
                per = 256 // ff_dev
                term[pl.ds(t * per, per)] = dot_nn(flip[...], grad[...]).reshape(per, ff_dev, D)
                return carry

            lax.fori_loop(0, FB // 256, term_out, 0, unroll=True)
            flip[...] = mixed[...].T
            term_o[...] = dot_nn(flip[...], grad[...]).reshape(R, rows, D)
            for j in range(J):
                for ref, m in ((keep, 2 * j), (send, 2 * j + 1)):
                    ref[j, :ff_dev] = term[br[1] ^ m].astype(ref.dtype)
                    ref[j, ff_dev:] = term_o[br[1] ^ m].astype(ref.dtype)

        keep_2, send_2 = call(
            terms_body, [("s", br)] + [("v", a) for a in (grad_r, hidden, mixed)],
            [sds((J, ff_dev + rows, D), F32), sds((J, ff_dev + rows, D), BF)],
            [pltpu.VMEM((R, ff_dev, D), F32), pltpu.VMEM((R, rows, D), F32), pltpu.VMEM((256, NT), BF)],
            flops=2 * NT * D * (FB + QB),
        )
        merged_2 = merge(keep_2, send_2)

        def total_body(x, live_ref, bo, own, p1, p2, out):
            y = x[...].astype(F32) + bo[...] + own[...] + p1[:T].astype(F32) + p2[...].astype(F32)
            out[...] = (y * live_ref[:T]).astype(BF)

        (block_out,) = call(
            total_body,
            [("v", a) for a in (block_in, live, bias_o, own_part, got_one, got_two)], [block],
        )

        def plane_1_body(br, *rest):
            got, (*outs, tot) = rest[: len(merged_1)], rest[len(merged_1) :]

            def total_of(part, low, high, width):
                y = 0.0
                for which, first in part:
                    y = y + got[which][low + first : high + first, :width].astype(F32)
                return y

            tot[:HALF] = total_of(lower, 0, HALF, W1)
            tot[HALF:] = total_of(upper, HALF, MA, W1)
            lines = total_of(upper, MA, MS, WO)
            for k, ref in enumerate(outs):
                ref[:rows] = tot[pl.ds(pl.multiple_of((br[0] ^ k) * rows, rows), rows)].astype(ref.dtype)
                y = jnp.sum(jnp.where(iota(lines.shape, 0) == (br[0] ^ k), lines, 0.0), axis=0, keepdims=True)
                ref[rows:, :WO] = jnp.broadcast_to(y, (8, WO)).astype(ref.dtype)

        z0, *zs = call(
            plane_1_body, [("s", br)] + [("v", a) for a in merged_1],
            [sds((rows + 8, W1), F32)] + [sds((rows + 8, W1), BF)] * 3, [pltpu.VMEM((MA, W1), F32)],
        )
        zs = [z0] + [across(z, k + 1) for k, z in enumerate(zs)]

        def plane_2_body(*rest):
            got, (w_out_ref, w_o_ref) = rest[:J], rest[J:]
            for ref, at in ((w_out_ref, slice(0, ff_dev)), (w_o_ref, slice(ff_dev, ff_dev + rows))):
                y = got[0][at]
                for other in got[1:]:
                    y = y + other[at].astype(F32)
                ref[...] = y

        grad_w_out, grad_w_o = call(
            plane_2_body, [("v", a) for a in merged_2], [sds((ff_dev, D), F32), sds((rows, D), F32)]
        )
        small_order = (0, 1, 2, 2, 3, 4, 5, 6)

        def input_body(x, grad, own, *rest):
            *parts, out = rest

            def fn(rws):
                centered, rstd = stats(x[rws].astype(F32))
                xh = centered * rstd
                g = own[rws]
                for ref in parts:
                    g = g + ref[: T].astype(F32)
                mean_g = jnp.mean(g, axis=-1, keepdims=True)
                mean_gx = jnp.mean(g * xh, axis=-1, keepdims=True)
                out[rws] = (grad[rws].astype(F32) + rstd * (g - mean_g - xh * mean_gx)).astype(BF)

            by_rows(T, T, fn)

        (grad_input,) = call(input_body, [("v", a) for a in (block_in, grad_r, own_g, *backs)], [block])

        def final_body(br, *rest):
            z, (w_in_ref, w_qkv_ref, *small_refs) = rest[:NB], rest[NB:]
            y = sum(ref[rows:, :WO].astype(F32) for ref in z)
            for ref, which in zip(small_refs, small_order):
                ref[...] = y[:1, out_offsets[which] : out_offsets[which] + out_widths[which]]
            for k, ref in enumerate(z):
                at = br[0] ^ k
                w_in_ref[:, lanes(at, FB)] = ref[:rows, 3 * QB :].astype(F32)
                for s in range(3):
                    w_qkv_ref[:, lanes(s * NB + at, QB)] = ref[:rows, s * QB : (s + 1) * QB].astype(F32)

        grad_w_in, grad_w_qkv, *outs = call(
            final_body, [("s", br)] + [("v", z) for z in zs],
            [sds((rows, NB * FB), F32), sds((rows, 3 * D), F32)] + [sds((1, out_widths[i]), F32) for i in small_order],
        )
        outs = [o.reshape(-1) for o in outs]

        grad_b_in, grad_b_qkv, grad_b_o, grad_b_out, grad_g1, grad_s1, grad_g2, grad_s2 = outs
        return (
            block_out, grad_input, grad_w_qkv, grad_b_qkv, grad_w_o, grad_b_o, grad_w_in, grad_b_in,
            grad_w_out, grad_b_out, grad_g1, grad_s1, grad_g2, grad_s2,
        )

    return on_device


def solution(mesh):
    two, one = P("dp", None), P("dp")
    n = mesh.shape["dp"]
    on_device = make(n)

    return jax.shard_map(
        on_device,
        mesh=mesh,
        in_specs=(two, two, two, one, two, one, two, one, two, one, one, one, one, one, P(), P(), P()),
        out_specs=(two, two, two, one, two, one, two, one, two, one, one, one, one, one),
        check_vma=False,
    )
```
